32 devices in a mesh: dp: 8 (over z, x), ctx: 4 (over y, core).
Axes of the slice: x: 2, y: 2, z: 4, core: 2. Of those that a mesh axis runs over, the one named last changes fastest.
Arguments:
- tokens: bfloat16 [64, 1024, 576], P('dp', 'ctx'), may hold values from -6 to 6
- w_qkv: bfloat16 [552960], P(('dp', 'ctx')), may hold values from -0.25 to 0.25
- w_out: bfloat16 [331776], P(('dp', 'ctx')), may hold values from -1 to 1
- w_gate_up: bfloat16 [1769472], P(('dp', 'ctx')), may hold values from -0.25 to 0.25
- w_down: bfloat16 [884736], P(('dp', 'ctx')), may hold values from -0.15625 to 0.15625
- gains: bfloat16 [1152], P(('dp', 'ctx')), may hold values from 0.099609375 to 1.8984375
- cotangent: bfloat16 [64, 1024, 576], P('dp', 'ctx'), may hold values from -6 to 6
Outputs:
- output: bfloat16 [64, 1024, 576], P('dp', 'ctx')
- grad_input: bfloat16 [64, 1024, 576], P('dp', 'ctx')
- grad_qkv: float32 [552960], P(('dp', 'ctx'))
- grad_out: float32 [331776], P(('dp', 'ctx'))
- grad_gate_up: float32 [1769472], P(('dp', 'ctx'))
- grad_down: float32 [884736], P(('dp', 'ctx'))
- grad_gains: float32 [1152], P(('dp', 'ctx'))
The draws below stay inside these ranges and needn't reach their ends.
All inputs are finite; a program needn't handle non-finite values.
Results may differ from the reference program's by a relative error of at most 0.014.
Values may be sent and summed in bfloat16 or wider, within the bound.
No kernel may reach another device: no remote copies, remote signals or barrier semaphores. Data moves between devices by JAX's collectives and lax.ppermute only.
A program may use at most 384 MiB of HBM per device.

```python
import math
import jax
import jax.numpy as jnp
from jax import lax

D = 576
HEADS = 9
KV_HEADS = 3
HEAD = 64
FF = 1536
LEN = 1024
QKVW = 960
BATCH = 64
N_CTX = 4


def shard_levels(rng, extent, shards, smallest, top_value):
    def one(dim, parts):
        heights = jax.random.uniform(jax.random.fold_in(jax.random.fold_in(rng, 6), dim), (parts,), jnp.float32, smallest / len(shards), top_value / len(shards))
        return jnp.repeat(jnp.exp(heights), extent[dim] // parts).reshape((-1,) + (1,) * (len(extent) - dim - 1))

    factor_of = one(*shards[0])
    for cut in shards[1:]:
        factor_of = factor_of * one(*cut)
    return factor_of


def bell_draw(stream_key, dims, scale, reach, cuts=(), dtype=jnp.bfloat16):
    loudness = shard_levels(stream_key, dims, cuts, -0.22, 0.18) if cuts else 1.0
    values = jax.random.normal(stream_key, dims, jnp.float32) * scale * loudness
    return jnp.minimum(jnp.maximum(values, -reach), reach).astype(dtype)


def setup_inputs(seed: int = 0) -> dict:
    seeds = jax.random.split(jax.random.key(seed), 8)
    tokens = bell_draw(seeds[0], (BATCH, LEN, D), 1.0, 6.0, ((0, 8), (1, 4)))
    w_qkv = bell_draw(seeds[1], (D * QKVW,), D ** -0.5, 0.25, ((0, 32),))
    w_out = bell_draw(seeds[2], (D * D,), (D // 16) ** -0.5, 1.0, ((0, 32),))
    w_gate_up = bell_draw(seeds[3], (2 * D * FF,), D ** -0.5, 0.25, ((0, 32),))
    w_down = bell_draw(seeds[4], (FF * D,), FF ** -0.5, 0.15625, ((0, 32),))
    gains = jnp.clip(1.0 + 0.18 * jax.random.normal(seeds[5], (2 * D,), jnp.float32), 0.099609375, 1.8984375).astype(jnp.bfloat16)
    cotangent = bell_draw(seeds[6], (BATCH, LEN, D), 1.0, 6.0, ((0, 8), (1, 4)))
    return {"tokens": tokens, "w_qkv": w_qkv, "w_out": w_out, "w_gate_up": w_gate_up, "w_down": w_down, "gains": gains, "cotangent": cotangent}


EPSILON = 1e-05
THETA_BASE = 100000.0
NEG_FILL = -1e+30
precise_mode = lax.Precision.HIGHEST

@jax.custom_vjp
def low(v):
    return lax.optimization_barrier(v.astype(jnp.bfloat16)).astype(jnp.float32)

@jax.custom_vjp
def low_back(v):
    return v

def low_keep(v):
    return (low(v), None)

def low_pass(kept, grad):
    return (grad,)

def back_keep(v):
    return (v, None)

def back_low(kept, grad):
    return (low(grad),)
low.defvjp(low_keep, low_pass)
low_back.defvjp(back_keep, back_low)

def angle_tables(positions, width):
    halves = jnp.arange(0, width, 2).astype(jnp.float32) / width
    inverse = jnp.exp(-math.log(THETA_BASE) * halves)
    angles = positions.astype(jnp.float32)[:, None] * inverse[None, :]
    angles = jnp.concatenate([angles, angles], axis=-1)
    return (jnp.cos(angles), jnp.sin(angles))

def rotate(values, cosine, sine):
    half = values.shape[-1] // 2
    turned = jnp.concatenate([-values[..., half:], values[..., :half]], axis=-1)
    return values * cosine + turned * sine

def rms_scale(values):
    return values * lax.rsqrt(lax.optimization_barrier(jnp.mean(values * values, axis=-1, keepdims=True)) + EPSILON)

def attend(block):
    queries, keys, values = block
    slices = queries.shape[1]
    piece = queries.shape[2]
    length = keys.shape[2]
    query_places = jnp.arange(slices)[:, None] * piece + jnp.arange(piece)[None, :]
    key_places = jnp.arange(length)
    allowed = query_places[:, :, None] >= key_places[None, None, :]
    scores = jnp.einsum('bjqhgd,bjkhd->bjhgqk', queries, keys, precision=precise_mode) * 0.125
    scores = low_back(jnp.where(allowed[None, :, None, None, :, :], scores, NEG_FILL))
    highest = lax.optimization_barrier(jnp.max(scores, axis=-1, keepdims=True))
    expo = jnp.exp(scores - highest)
    probs = low(expo / lax.optimization_barrier(jnp.sum(expo, axis=-1, keepdims=True)))
    mixed = jnp.einsum('bjhgqk,bjkhd->bjqhgd', probs, values, precision=precise_mode)
    return low(low_back(mixed))

def block_count(batch, length):
    per_block = min(batch, max(1, 4096 // length))
    while batch % per_block:
        per_block = per_block - 1
    return per_block

def forward(inputs, wqkv_flat, wout_flat, wgu_flat, wdown_flat, gain_pair):
    batch = inputs.shape[0]
    length = inputs.shape[1]
    group = HEADS // KV_HEADS
    kv_width = KV_HEADS * HEAD
    piece = length // N_CTX
    mat_qkv = wqkv_flat.reshape(D, QKVW)
    mat_out = wout_flat.reshape(D, D)
    mat_gu = wgu_flat.reshape(D, 2 * FF)
    mat_down = wdown_flat.reshape(FF, D)
    rows = inputs.reshape(batch * length, D)
    normed_one = low(rms_scale(rows) * gain_pair[:D])
    projected = low_back(jnp.dot(normed_one, mat_qkv, precision=precise_mode))
    cosine, sine = angle_tables(jnp.arange(length), HEAD)
    queries = projected[:, :D].reshape(batch, length, HEADS, HEAD)
    keys = projected[:, D:D + kv_width].reshape(batch, length, KV_HEADS, HEAD)
    values = projected[:, D + kv_width:].reshape(batch, length, KV_HEADS, HEAD)
    queries = low(rotate(queries, cosine[None, :, None, :], sine[None, :, None, :]))
    queries = queries.reshape(batch, N_CTX, piece, KV_HEADS, group, HEAD)
    key_copies = low_back(jnp.broadcast_to(keys[:, None], (batch, N_CTX, length, KV_HEADS, HEAD)))
    key_copies = low(rotate(key_copies, cosine[None, None, :, None, :], sine[None, None, :, None, :]))
    value_copies = low_back(jnp.broadcast_to(low(values)[:, None], (batch, N_CTX, length, KV_HEADS, HEAD)))
    per_block = block_count(batch, length)
    blocks = batch // per_block

    def shaped(array):
        return array.reshape((blocks, per_block) + array.shape[1:])
    mixed = lax.map(jax.checkpoint(attend), (shaped(queries), shaped(key_copies), shaped(value_copies)))
    mixed = mixed.reshape(batch * length, D)
    branch = low_back(jnp.dot(mixed, mat_out, precision=precise_mode))
    residual = rows + branch
    normed_two = low(rms_scale(residual) * gain_pair[D:])
    gate_up = low_back(jnp.dot(normed_two, mat_gu, precision=precise_mode))
    gate_part = gate_up[:, :FF]
    up_part = gate_up[:, FF:]
    activated = low(gate_part / (1.0 + jnp.exp(-gate_part)) * up_part)
    out_branch = low_back(jnp.dot(activated, mat_down, precision=precise_mode))
    return (residual + out_branch).reshape(batch, length, D)

def reference(tokens, w_qkv, w_out, w_gate_up, w_down, gains, cotangent):
    result, puller = jax.vjp(forward, tokens.astype(jnp.float32), w_qkv.astype(jnp.float32), w_out.astype(jnp.float32), w_gate_up.astype(jnp.float32), w_down.astype(jnp.float32), gains.astype(jnp.float32))
    grads = puller(cotangent.astype(jnp.float32))
    return (result.astype(jnp.bfloat16), grads[0].astype(jnp.bfloat16), grads[1], grads[2], grads[3], grads[4], grads[5])
```

```python
import math

import jax
import jax.numpy as jnp
from jax import lax
from jax.experimental import pallas as pl
from jax.experimental.pallas import tpu as pltpu
from jax.sharding import PartitionSpec as P

D = 576
HEADS = 9
KV_HEADS = 3
HEAD = 64
FF = 1536
QKVW = 960
KV0 = D
V0 = D + KV_HEADS * HEAD
HALF = HEAD // 2
TILE = 256

EPSILON = 1e-05
THETA_BASE = 100000.0
NEG_FILL = -1e30
BF = jnp.bfloat16
F32 = jnp.float32


def nn(a, b):
    return lax.dot_general(a, b, (((1,), (0,)), ((), ())), preferred_element_type=F32)


def nt(a, b):
    return lax.dot_general(a, b, (((1,), (1,)), ((), ())), preferred_element_type=F32)


def eye(size):
    r = lax.broadcasted_iota(jnp.int32, (size, size), 0)
    c = lax.broadcasted_iota(jnp.int32, (size, size), 1)
    return jnp.where(r == c, 1.0, 0.0).astype(BF)


def col_chunks(width, step=128):
    return [(c, min(step, width - c)) for c in range(0, width, step)]


def flip(rows):
    parts = [nt(eye(w), rows[:, c : c + w]).astype(BF) for c, w in col_chunks(rows.shape[1])]
    return jnp.concatenate(parts, axis=0)


def unflip(cols):
    return nt(eye(cols.shape[1]), cols).astype(BF)


def inverse_rms(cols):
    return lax.rsqrt(jnp.sum(cols * cols, axis=0, keepdims=True) * (1.0 / D) + EPSILON)


def rotary_tables(length):
    halves = jnp.arange(0, HEAD, 2).astype(F32) / HEAD
    inverse = jnp.exp(-math.log(THETA_BASE) * halves)
    angles = inverse[:, None] * jnp.arange(length).astype(F32)[None, :]
    return jnp.cos(angles), jnp.sin(angles)


def tri_mask(size):
    key = lax.broadcasted_iota(jnp.int32, (size, size), 0)
    query = lax.broadcasted_iota(jnp.int32, (size, size), 1)
    return key <= query


def forward_kernel(me_ref, x_ref, wt_ref, gain_ref, cos_ref, sin_ref, xt_ref, qkv_ref, o_ref, lse_ref, krow):
    slices, _, span, _ = x_ref.shape
    length = slices * span
    me = me_ref[0]
    for k in range(slices):
        at = pl.multiple_of((me ^ k) * span, span)
        xt_ref[0, :, pl.ds(at, span)] = flip(x_ref[k, 0])
    gain = gain_ref[...]
    wt = wt_ref[...]
    for t in range(0, length, TILE):
        x = xt_ref[0, :, t : t + TILE].astype(F32)
        normed = (x * inverse_rms(x) * gain).astype(BF)
        proj = nn(wt, normed)
        cos = cos_ref[:, t : t + TILE]
        sin = sin_ref[:, t : t + TILE]
        for j in range(HEADS + KV_HEADS):
            u1 = proj[j * HEAD : j * HEAD + HALF]
            u2 = proj[j * HEAD + HALF : (j + 1) * HEAD]
            r1 = (u1 * cos - u2 * sin).astype(BF)
            r2 = (u2 * cos + u1 * sin).astype(BF)
            if j < HEADS:
                r1 = r1 * jnp.asarray(0.125, BF)
                r2 = r2 * jnp.asarray(0.125, BF)
            qkv_ref[0, j * HEAD : j * HEAD + HALF, t : t + TILE] = r1
            qkv_ref[0, j * HEAD + HALF : (j + 1) * HEAD, t : t + TILE] = r2
        qkv_ref[0, V0:, t : t + TILE] = proj[V0:].astype(BF)
        for j in range(KV_HEADS):
            krow[j, t : t + TILE, :] = unflip(qkv_ref[0, KV0 + j * HEAD : KV0 + (j + 1) * HEAD, t : t + TILE])

    keep = tri_mask(TILE)

    def head(h, carry):
        kv = h // (HEADS // KV_HEADS)
        rows = pl.ds(pl.multiple_of(h * HEAD, HEAD), HEAD)
        vrows = pl.ds(pl.multiple_of(V0 + kv * HEAD, HEAD), HEAD)
        for t in range(0, length, TILE):
            cols = slice(t, t + TILE)
            q = qkv_ref[0, rows, cols]
            last = jnp.where(keep, nn(krow[kv, cols, :], q), NEG_FILL)
            top = jnp.max(last, axis=0, keepdims=True)
            if t:
                before = nn(krow[kv, 0:t, :], q)
                top = jnp.maximum(top, jnp.max(before, axis=0, keepdims=True))
            e = jnp.exp(last - top)
            total = jnp.sum(e, axis=0, keepdims=True)
            acc = nn(qkv_ref[0, vrows, cols], e.astype(BF))
            if t:
                e = jnp.exp(before - top)
                total = total + jnp.sum(e, axis=0, keepdims=True)
                acc = acc + nn(qkv_ref[0, vrows, 0:t], e.astype(BF))
            o_ref[0, rows, cols] = (acc * (1.0 / total)).astype(BF)
            lse_ref[0, pl.ds(h, 1), cols] = top + jnp.log(total)
        return carry

    lax.fori_loop(0, HEADS, head, 0)


def middle_kernel(
    me_ref, xt_ref, o_ref, dy_ref, wo_ref, wgu_ref, wd_ref, gain_ref,
    out_ref, dr_ref, do_ref, delta_ref, gout_ref, ggu_ref, gdown_ref, gg_ref,
    wot, wgut, wdt, aout, agu, adown,
):
    step = pl.program_id(0) * pl.num_programs(1) + pl.program_id(1)
    last = pl.num_programs(0) * pl.num_programs(1) - 1

    @pl.when(step == 0)
    def _():
        for c in range(0, 2 * FF, TILE):
            wgut[c : c + TILE, :] = nt(eye(TILE), wgu_ref[:, c : c + TILE]).astype(BF)
        for c, w in col_chunks(D):
            wdt[c : c + w, :] = nt(eye(w), wd_ref[:, c : c + w]).astype(BF)
            wot[c : c + w, :] = nt(eye(w), wo_ref[:, c : c + w]).astype(BF)
        aout[...] = jnp.zeros_like(aout)
        agu[...] = jnp.zeros_like(agu)
        adown[...] = jnp.zeros_like(adown)
        gg_ref[...] = jnp.zeros_like(gg_ref)

    gain = gain_ref[...]
    o = o_ref[0]
    r = xt_ref[0].astype(F32) + nn(wot[...], o)
    inv = inverse_rms(r)
    n = r * inv
    h = (n * gain).astype(BF)
    a = nn(wgut[0:FF, :], h)
    u = nn(wgut[FF:, :], h)
    sg = 1.0 / (1.0 + jnp.exp(-a))
    act = a * sg
    m = (act * u).astype(BF)
    out_ref[0, 0] = unflip((r + nn(wdt[...], m)).astype(BF))
    dy = dy_ref[0, 0]
    dyt = flip(dy)
    adown[...] += nn(m, dy)
    dm = nn(wd_ref[...], dyt)
    da = (dm * u * sg * (1.0 + a * (1.0 - sg))).astype(BF)
    du = (dm * act).astype(BF)
    agu[:, 0:FF] += nt(h, da)
    agu[:, FF:] += nt(h, du)
    dh = nn(wgu_ref[:, 0:FF], da) + nn(wgu_ref[:, FF:], du)
    dhn = dh * n
    part = dhn[:, 0:128]
    for c in range(128, dhn.shape[1], 128):
        part = part + dhn[:, c : c + 128]
    gg_ref[...] += part
    e = dh * gain
    dr = dyt.astype(F32) + inv * (e - n * (jnp.sum(e * n, axis=0, keepdims=True) * (1.0 / D)))
    dr_ref[0] = dr
    db = dr.astype(BF)
    aout[...] += nt(o, db)
    do = nn(wo_ref[...], db).astype(BF)
    do_ref[0] = do
    prod = do.astype(F32) * o.astype(F32)
    for j in range(HEADS):
        delta_ref[0, j : j + 1, :] = jnp.sum(prod[j * HEAD : (j + 1) * HEAD], axis=0, keepdims=True)

    @pl.when(step == last)
    def _():
        gout_ref[...] = aout[...].astype(BF)
        ggu_ref[...] = agu[...].astype(BF)
        gdown_ref[...] = adown[...].astype(BF)


def backward_kernel(
    me_ref, xt_ref, qkv_ref, do_ref, lse_ref, delta_ref, dr_ref, w_ref, gain_ref, cos_ref, sin_ref,
    gin_ref, gqkv_ref, gg_ref,
    krow, vrow, grads, acc,
):
    slices, _, span, _ = gin_ref.shape
    length = slices * span
    me = me_ref[0]

    @pl.when(pl.program_id(0) == 0)
    def _():
        acc[...] = jnp.zeros_like(acc)
        gg_ref[...] = jnp.zeros_like(gg_ref)

    grads[...] = jnp.zeros_like(grads)
    for t in range(0, length, TILE):
        for j in range(KV_HEADS):
            krow[j, t : t + TILE, :] = unflip(qkv_ref[0, KV0 + j * HEAD : KV0 + (j + 1) * HEAD, t : t + TILE])
            vrow[j, t : t + TILE, :] = unflip(qkv_ref[0, V0 + j * HEAD : V0 + (j + 1) * HEAD, t : t + TILE])

    keep = tri_mask(TILE)

    def head(h, carry):
        kv = h // (HEADS // KV_HEADS)
        rows = pl.ds(pl.multiple_of(h * HEAD, HEAD), HEAD)
        krows = pl.ds(pl.multiple_of(KV0 + kv * HEAD, HEAD), HEAD)
        vrows = pl.ds(pl.multiple_of(V0 + kv * HEAD, HEAD), HEAD)
        for t in range(0, length, TILE):
            cols = slice(t, t + TILE)
            q = qkv_ref[0, rows, cols]
            do = do_ref[0, rows, cols]
            lse = lse_ref[0, pl.ds(h, 1), cols]
            delta = delta_ref[0, pl.ds(h, 1), cols]
            p = jnp.where(keep, jnp.exp(nn(krow[kv, cols, :], q) - lse), 0.0)
            ds = (p * (nn(vrow[kv, cols, :], do) - delta)).astype(BF)
            grads[vrows, cols] += nt(do, p.astype(BF))
            grads[krows, cols] += nt(q, ds)
            dq = nn(qkv_ref[0, krows, cols], ds)
            if t:
                p = jnp.exp(nn(krow[kv, 0:t, :], q) - lse)
                ds = (p * (nn(vrow[kv, 0:t, :], do) - delta)).astype(BF)
                grads[vrows, 0:t] += nt(do, p.astype(BF))
                grads[krows, 0:t] += nt(q, ds)
                dq = dq + nn(qkv_ref[0, krows, 0:t], ds)
            grads[rows, cols] = dq * 0.125
        return carry

    lax.fori_loop(0, HEADS, head, 0)

    gain = gain_ref[...]
    w = w_ref[...]
    for k in range(slices):
        at = pl.multiple_of((me ^ k) * span, span)
        cols = pl.ds(at, span)
        cos = cos_ref[:, cols]
        sin = sin_ref[:, cols]
        parts = []
        for j in range(HEADS + KV_HEADS):
            g1 = grads[j * HEAD : j * HEAD + HALF, cols]
            g2 = grads[j * HEAD + HALF : (j + 1) * HEAD, cols]
            parts.append((g1 * cos + g2 * sin).astype(BF))
            parts.append((g2 * cos - g1 * sin).astype(BF))
        parts.append(grads[V0:, cols].astype(BF))
        dp = jnp.concatenate(parts, axis=0)
        x = xt_ref[0, :, cols].astype(F32)
        inv = inverse_rms(x)
        n = x * inv
        normed = (n * gain).astype(BF)
        acc[...] += nt(normed, dp)
        dh = nn(w, dp)
        dhn = dh * n
        part = dhn[:, 0:128]
        for c in range(128, span, 128):
            part = part + dhn[:, c : c + 128]
        gg_ref[...] += part
        e = dh * gain
        gin = dr_ref[0, :, cols] + inv * (e - n * (jnp.sum(e * n, axis=0, keepdims=True) * (1.0 / D)))
        gin_ref[k, 0] = unflip(gin.astype(BF))

    @pl.when(pl.program_id(0) == pl.num_programs(0) - 1)
    def _():
        gqkv_ref[...] = acc[...].astype(BF)


WHOLE = pl.BlockSpec(memory_space=pltpu.VMEM)


def attention_forward(me, x_stack, wt, gain, cos, sin):
    slices, seqs, span, _ = x_stack.shape
    length = slices * span
    by_seq = lambda rows: pl.BlockSpec((1, rows, length), lambda s, me: (s, 0, 0))
    return pl.pallas_call(
        forward_kernel,
        grid_spec=pltpu.PrefetchScalarGridSpec(
            num_scalar_prefetch=1,
            grid=(seqs,),
            in_specs=[
                pl.BlockSpec((slices, 1, span, D), lambda s, me: (0, s, 0, 0)),
                WHOLE, WHOLE, WHOLE, WHOLE,
            ],
            out_specs=[by_seq(D), by_seq(QKVW), by_seq(D), by_seq(HEADS)],
            scratch_shapes=[pltpu.VMEM((KV_HEADS, length, HEAD), BF)],
        ),
        out_shape=[
            jax.ShapeDtypeStruct((seqs, D, length), BF),
            jax.ShapeDtypeStruct((seqs, QKVW, length), BF),
            jax.ShapeDtypeStruct((seqs, D, length), BF),
            jax.ShapeDtypeStruct((seqs, HEADS, length), F32),
        ],
        compiler_params=pltpu.CompilerParams(vmem_limit_bytes=48 << 20),
        cost_estimate=pl.CostEstimate(
            flops=seqs * (2 * length * D * QKVW + 6 * HEADS * length * length * HEAD),
            bytes_accessed=seqs * length * 7000,
            transcendentals=seqs * HEADS * length * length // 2,
        ),
        name="attention_forward",
    )(me, x_stack, wt, gain, cos, sin)


def middle(me, xt, o, dy_stack, wo, wgu, wd, gain):
    slices, seqs, span, _ = dy_stack.shape
    length = slices * span
    tile = lambda rows: pl.BlockSpec((1, rows, span), lambda s, k, me: (s, 0, k ^ me[0]))
    stacked = pl.BlockSpec((1, 1, span, D), lambda s, k, me: (k, s, 0, 0))
    return pl.pallas_call(
        middle_kernel,
        grid_spec=pltpu.PrefetchScalarGridSpec(
            num_scalar_prefetch=1,
            grid=(seqs, slices),
            in_specs=[tile(D), tile(D), stacked, WHOLE, WHOLE, WHOLE, WHOLE],
            out_specs=[stacked, tile(D), tile(D), tile(HEADS), WHOLE, WHOLE, WHOLE, WHOLE],
            scratch_shapes=[
                pltpu.VMEM((D, D), BF),
                pltpu.VMEM((2 * FF, D), BF),
                pltpu.VMEM((D, FF), BF),
                pltpu.VMEM((D, D), F32),
                pltpu.VMEM((D, 2 * FF), F32),
                pltpu.VMEM((FF, D), F32),
            ],
        ),
        out_shape=[
            jax.ShapeDtypeStruct((slices, seqs, span, D), BF),
            jax.ShapeDtypeStruct((seqs, D, length), F32),
            jax.ShapeDtypeStruct((seqs, D, length), BF),
            jax.ShapeDtypeStruct((seqs, HEADS, length), F32),
            jax.ShapeDtypeStruct((D, D), BF),
            jax.ShapeDtypeStruct((D, 2 * FF), BF),
            jax.ShapeDtypeStruct((FF, D), BF),
            jax.ShapeDtypeStruct((D, 128), F32),
        ],
        compiler_params=pltpu.CompilerParams(vmem_limit_bytes=60 << 20),
        cost_estimate=pl.CostEstimate(
            flops=seqs * length * 6 * (D * D + 3 * D * FF),
            bytes_accessed=seqs * length * 8000 + 12000000,
            transcendentals=seqs * length * FF,
        ),
        name="middle",
    )(me, xt, o, dy_stack, wo, wgu, wd, gain)


def attention_backward(me, xt, qkv, do, lse, delta, dr, w, gain, cos, sin, slices):
    seqs, _, length = xt.shape
    span = length // slices
    by_seq = lambda rows: pl.BlockSpec((1, rows, length), lambda s, me: (s, 0, 0))
    return pl.pallas_call(
        backward_kernel,
        grid_spec=pltpu.PrefetchScalarGridSpec(
            num_scalar_prefetch=1,
            grid=(seqs,),
            in_specs=[
                by_seq(D), by_seq(QKVW), by_seq(D), by_seq(HEADS), by_seq(HEADS), by_seq(D),
                WHOLE, WHOLE, WHOLE, WHOLE,
            ],
            out_specs=[
                pl.BlockSpec((slices, 1, span, D), lambda s, me: (0, s, 0, 0)),
                WHOLE, WHOLE,
            ],
            scratch_shapes=[
                pltpu.VMEM((KV_HEADS, length, HEAD), BF),
                pltpu.VMEM((KV_HEADS, length, HEAD), BF),
                pltpu.VMEM((QKVW, length), F32),
                pltpu.VMEM((D, QKVW), F32),
            ],
        ),
        out_shape=[
            jax.ShapeDtypeStruct((slices, seqs, span, D), BF),
            jax.ShapeDtypeStruct((D, QKVW), BF),
            jax.ShapeDtypeStruct((D, 128), F32),
        ],
        compiler_params=pltpu.CompilerParams(vmem_limit_bytes=56 << 20),
        cost_estimate=pl.CostEstimate(
            flops=seqs * (4 * length * D * QKVW + 10 * HEADS * length * length * HEAD),
            bytes_accessed=seqs * length * 9000,
            transcendentals=seqs * HEADS * length * length // 2,
        ),
        name="attention_backward",
    )(me, xt, qkv, do, lse, delta, dr, w, gain, cos, sin)


def local(tokens, w_qkv, w_out, w_gate_up, w_down, gains, cotangent):
    both = ("dp", "ctx")
    slices = lax.axis_size("ctx")
    world = slices * lax.axis_size("dp")
    span = tokens.shape[1]
    seqs = tokens.shape[0] // slices
    length = slices * span
    me = jnp.zeros((1,), jnp.int32)

    def swap(array):
        return lax.all_to_all(array, "ctx", split_axis=0, concat_axis=0, tiled=True)

    def scatter_sum(terms):
        terms = jnp.pad(terms, ((0, 0), (0, -terms.shape[1] % 128)))
        return lax.psum_scatter(
            terms.reshape(world, -1, 128), both, scatter_dimension=0, tiled=True
        ).reshape(-1)

    first = lax.all_gather(jnp.concatenate([w_qkv, gains]), both, axis=0, tiled=False)
    mat_qkv = first[:, : w_qkv.shape[0]].reshape(D, QKVW)
    gain_all = first[:, w_qkv.shape[0] :].reshape(2, D, 1).astype(F32)
    x_stack = swap(tokens).reshape(slices, seqs, span, D)
    rest = lax.all_gather(jnp.concatenate([w_out, w_gate_up, w_down]), both, axis=0, tiled=False)
    c1 = w_out.shape[0]
    c2 = c1 + w_gate_up.shape[0]
    mat_out = rest[:, :c1].reshape(D, D)
    mat_gu = rest[:, c1:c2].reshape(D, 2 * FF)
    mat_down = rest[:, c2:].reshape(FF, D)
    cos, sin = rotary_tables(length)
    xt, qkv, o, lse = attention_forward(me, x_stack, mat_qkv.T, gain_all[0], cos, sin)
    dy_stack = swap(cotangent).reshape(slices, seqs, span, D)
    out_stack, dr, do, delta, g_out, g_gu, g_down, gg2 = middle(
        me, xt, o, dy_stack, mat_out, mat_gu, mat_down, gain_all[1]
    )
    output = swap(out_stack.reshape(slices * seqs, span, D))
    packed = jnp.concatenate(
        [g_out.reshape(world, -1), g_gu.reshape(world, -1), g_down.reshape(world, -1)], axis=1
    )
    owned = scatter_sum(packed)
    gin_stack, g_qkv, gg1 = attention_backward(
        me, xt, qkv, do, lse, delta, dr, mat_qkv, gain_all[0], cos, sin, slices
    )
    grad_input = swap(gin_stack.reshape(slices * seqs, span, D))
    gg = jnp.concatenate([jnp.sum(gg1, axis=1), jnp.sum(gg2, axis=1)]).astype(BF)
    late = jnp.concatenate([g_qkv.reshape(world, -1), gg.reshape(world, -1)], axis=1)
    owned_late = scatter_sum(late)
    n_qkv = w_qkv.shape[0]
    return (
        output,
        grad_input,
        owned_late[:n_qkv].astype(F32),
        owned[:c1].astype(F32),
        owned[c1:c2].astype(F32),
        owned[c2 : c2 + w_down.shape[0]].astype(F32),
        owned_late[n_qkv : n_qkv + gains.shape[0]].astype(F32),
    )


def solution(mesh):
    flat = P(("dp", "ctx"))
    rows = P("dp", "ctx", None)
    return jax.shard_map(
        local,
        mesh=mesh,
        in_specs=(rows, flat, flat, flat, flat, flat, rows),
        out_specs=(rows, rows, flat, flat, flat, flat, flat),
        check_vma=False,
    )
```

```python
import functools
import math

import jax
import jax.numpy as jnp
from jax import lax
from jax.experimental import pallas as pl
from jax.experimental.pallas import tpu as pltpu
from jax.sharding import PartitionSpec as P

D = 576
HEADS = 9
KV_HEADS = 3
HEAD = 64
FF = 1536
QKVW = 960
KV0 = D
V0 = D + KV_HEADS * HEAD
HALF = HEAD // 2
TILE = 256

EPSILON = 1e-05
THETA_BASE = 100000.0
NEG_FILL = -1e30
BF = jnp.bfloat16
F32 = jnp.float32


def nn(a, b):
    return lax.dot_general(a, b, (((1,), (0,)), ((), ())), preferred_element_type=F32)


def nt(a, b):
    return lax.dot_general(a, b, (((1,), (1,)), ((), ())), preferred_element_type=F32)


def eye(size):
    r = lax.broadcasted_iota(jnp.int32, (size, size), 0)
    c = lax.broadcasted_iota(jnp.int32, (size, size), 1)
    return jnp.where(r == c, 1.0, 0.0).astype(BF)


def col_chunks(width, step=128):
    return [(c, min(step, width - c)) for c in range(0, width, step)]


def flip(rows):
    parts = [nt(eye(w), rows[:, c : c + w]).astype(BF) for c, w in col_chunks(rows.shape[1])]
    return jnp.concatenate(parts, axis=0)


def unflip(cols):
    return nt(eye(cols.shape[1]), cols).astype(BF)


def inverse_rms(cols):
    return lax.rsqrt(jnp.sum(cols * cols, axis=0, keepdims=True) * (1.0 / D) + EPSILON)


def rotary_tables(length):
    halves = jnp.arange(0, HEAD, 2).astype(F32) / HEAD
    inverse = jnp.exp(-math.log(THETA_BASE) * halves)
    angles = inverse[:, None] * jnp.arange(length).astype(F32)[None, :]
    return jnp.cos(angles), jnp.sin(angles)


def tri_mask(size):
    key = lax.broadcasted_iota(jnp.int32, (size, size), 0)
    query = lax.broadcasted_iota(jnp.int32, (size, size), 1)
    return key <= query


def lane_low(size):
    return lax.broadcasted_iota(jnp.int32, (size, 128), 1) < 64


def to_flat(rows_ref, flat_ref, rows, width):
    if width % 128 == 0:
        n = width // 128

        @pl.loop(0, n)
        def _(c):
            flat_ref[pl.ds(c, rows, stride=n), :] = rows_ref[:, pl.ds(pl.multiple_of(c * 128, 128), 128)]

        return
    n = 2 * width // 128
    half = rows // 2
    low = lane_low(half)
    even = lambda c: rows_ref[c, pl.ds(0, half, stride=2), :]
    odd = lambda c: pltpu.roll(rows_ref[c, pl.ds(1, half, stride=2), :], 64, 1)
    for c in range(n // 2):
        flat_ref[pl.ds(c, half, stride=n), :] = even(c)
    before = odd(0)
    flat_ref[pl.ds(n // 2, half, stride=n), :] = jnp.where(low, even(n // 2), before)
    for c in range(n // 2):
        after = odd(c + 1)
        flat_ref[pl.ds(n // 2 + 1 + c, half, stride=n), :] = jnp.where(low, before, after)
        before = after


def from_flat(flat_ref, rows_ref, rows, width):
    if width % 128 == 0:
        n = width // 128

        @pl.loop(0, n)
        def _(c):
            rows_ref[:, pl.ds(pl.multiple_of(c * 128, 128), 128)] = flat_ref[
                pl.ds(c, rows, stride=n), :
            ].astype(rows_ref.dtype)

        return
    n = 2 * width // 128
    half = rows // 2
    low = lane_low(half)
    take = lambda c: flat_ref[pl.ds(c, half, stride=n), :]
    for c in range(n // 2 + 1):
        rows_ref[c, pl.ds(0, half, stride=2), :] = take(c)
    before = pltpu.roll(take(n // 2), 64, 1)
    for c in range(n // 2):
        after = pltpu.roll(take(n // 2 + 1 + c), 64, 1)
        rows_ref[c, pl.ds(1, half, stride=2), :] = jnp.where(low, before, after)
        before = after
    rows_ref[n // 2, pl.ds(1, half, stride=2), :] = before


def convert(src_ref, dst_ref, rows, step):
    @pl.loop(0, rows, step=step)
    def _(i):
        at = pl.ds(pl.multiple_of(i, step), step)
        dst_ref[at, :] = src_ref[at, 0 : dst_ref.shape[1]].astype(dst_ref.dtype)


def clear(ref, step):
    @pl.loop(0, ref.shape[-2], step=step)
    def _(i):
        at = pl.ds(pl.multiple_of(i, step), step)
        if len(ref.shape) == 3:
            ref[:, at, :] = jnp.zeros((ref.shape[0], step, ref.shape[2]), ref.dtype)
        else:
            ref[at, :] = jnp.zeros((step, ref.shape[1]), ref.dtype)


def add_chunks(ref, value):
    for c, w in col_chunks(value.shape[1]):
        ref[c // 128, :, 0:w] += value[:, c : c + w]


def join_chunks(src_ref, dst_ref):
    for c, w in col_chunks(dst_ref.shape[1]):
        dst_ref[:, c : c + w] = src_ref[c // 128, :, 0:w].astype(dst_ref.dtype)


def forward_kernel(slices, me_ref, *refs):
    x_refs = refs[:slices]
    wt_ref, gain_ref, cos_ref, sin_ref, xt_ref, qkv_ref, o_ref, lse_ref, krow = refs[slices:]
    _, span, _ = x_refs[0].shape
    length = slices * span
    me = me_ref[0]
    for k in range(slices):
        at = pl.multiple_of((me ^ k) * span, span)
        xt_ref[0, :, pl.ds(at, span)] = flip(x_refs[k][0])
    gain = gain_ref[...]

    @pl.loop(0, length, step=TILE)
    def _(start):
        tok = pl.ds(pl.multiple_of(start, TILE), TILE)
        x = xt_ref[0, :, tok].astype(F32)
        normed = (x * inverse_rms(x) * gain).astype(BF)
        proj = nn(wt_ref[...], normed)
        cos = cos_ref[:, tok]
        sin = sin_ref[:, tok]
        for j in range(HEADS + KV_HEADS):
            u1 = proj[j * HEAD : j * HEAD + HALF]
            u2 = proj[j * HEAD + HALF : (j + 1) * HEAD]
            r1 = (u1 * cos - u2 * sin).astype(BF)
            r2 = (u2 * cos + u1 * sin).astype(BF)
            if j < HEADS:
                r1 = r1 * jnp.asarray(0.125, BF)
                r2 = r2 * jnp.asarray(0.125, BF)
            qkv_ref[0, j * HEAD : j * HEAD + HALF, tok] = r1
            qkv_ref[0, j * HEAD + HALF : (j + 1) * HEAD, tok] = r2
        qkv_ref[0, V0:, tok] = proj[V0:].astype(BF)
        for j in range(KV_HEADS):
            krow[j, tok, :] = unflip(qkv_ref[0, KV0 + j * HEAD : KV0 + (j + 1) * HEAD, tok])

    keep = tri_mask(TILE)

    def head(h, carry):
        kv = h // (HEADS // KV_HEADS)
        rows = pl.ds(pl.multiple_of(h * HEAD, HEAD), HEAD)
        vrows = pl.ds(pl.multiple_of(V0 + kv * HEAD, HEAD), HEAD)
        for t in range(0, length, TILE):
            cols = slice(t, t + TILE)
            q = qkv_ref[0, rows, cols]
            last = jnp.where(keep, nn(krow[kv, cols, :], q), NEG_FILL)
            top = jnp.max(last, axis=0, keepdims=True)
            if t:
                before = nn(krow[kv, 0:t, :], q)
                top = jnp.maximum(top, jnp.max(before, axis=0, keepdims=True))
            e = jnp.exp(last - top)
            total = jnp.sum(e, axis=0, keepdims=True)
            acc = nn(qkv_ref[0, vrows, cols], e.astype(BF))
            if t:
                e = jnp.exp(before - top)
                total = total + jnp.sum(e, axis=0, keepdims=True)
                acc = acc + nn(qkv_ref[0, vrows, 0:t], e.astype(BF))
            o_ref[0, rows, cols] = (acc * (1.0 / total)).astype(BF)
            lse_ref[0, pl.ds(h, 1), cols] = top + jnp.log(total)
        return carry

    lax.fori_loop(0, HEADS, head, 0)


def middle_kernel(
    me_ref, xt_ref, o_ref, dy_ref, fo_ref, fgu_ref, fd_ref, gain_ref,
    out_ref, dr_ref, do_ref, delta_ref, gout_ref, ggu_ref, gdown_ref, gg_ref,
    wo_ref, wgu_ref, wd_ref, wot, wgut, wdt, aout, agu, adown,
):
    step = pl.program_id(0) * pl.num_programs(1) + pl.program_id(1)
    last = pl.num_programs(0) * pl.num_programs(1) - 1

    @pl.when(step == 0)
    def _():
        convert(fgu_ref, ggu_ref, fgu_ref.shape[0], 256)
        from_flat(ggu_ref, wgu_ref, D, 2 * FF)
        convert(fd_ref, gdown_ref, fd_ref.shape[0], 256)
        from_flat(gdown_ref, adown, FF, D)
        join_chunks(adown, wd_ref)
        convert(fo_ref, gout_ref, fo_ref.shape[0], 96)
        from_flat(gout_ref, aout, D, D)
        join_chunks(aout, wo_ref)

        @pl.loop(0, 2 * FF, step=TILE)
        def _(c):
            at = pl.ds(pl.multiple_of(c, TILE), TILE)
            wgut[at, :] = nt(eye(TILE), wgu_ref[:, at]).astype(BF)

        for c, w in col_chunks(D):
            wdt[c : c + w, :] = nt(eye(w), wd_ref[:, c : c + w]).astype(BF)
            wot[c : c + w, :] = nt(eye(w), wo_ref[:, c : c + w]).astype(BF)
        clear(aout, 64)
        clear(agu, 16)
        clear(adown, 64)
        gg_ref[...] = jnp.zeros_like(gg_ref)

    gain = gain_ref[...]
    o = o_ref[0]
    r = xt_ref[0].astype(F32) + nn(wot[...], o)
    inv = inverse_rms(r)
    n = r * inv
    h = (n * gain).astype(BF)
    a = nn(wgut[0:FF, :], h)
    u = nn(wgut[FF:, :], h)
    sg = 1.0 / (1.0 + jnp.exp(-a))
    act = a * sg
    m = (act * u).astype(BF)
    out_ref[0, 0] = unflip((r + nn(wdt[...], m)).astype(BF))
    dy = dy_ref[0, 0]
    dyt = flip(dy)
    add_chunks(adown, nn(m, dy))
    dm = nn(wd_ref[...], dyt)
    da = (dm * u * sg * (1.0 + a * (1.0 - sg))).astype(BF)
    du = (dm * act).astype(BF)
    agu[:, 0:FF] += nt(h, da)
    agu[:, FF:] += nt(h, du)
    dh = nn(wgu_ref[:, 0:FF], da) + nn(wgu_ref[:, FF:], du)
    dhn = dh * n
    part = dhn[:, 0:128]
    for c in range(128, dhn.shape[1], 128):
        part = part + dhn[:, c : c + 128]
    gg_ref[...] += part
    e = dh * gain
    dr = dyt.astype(F32) + inv * (e - n * (jnp.sum(e * n, axis=0, keepdims=True) * (1.0 / D)))
    dr_ref[0] = dr
    db = dr.astype(BF)
    add_chunks(aout, nt(o, db))
    do = nn(wo_ref[...], db).astype(BF)
    do_ref[0] = do
    prod = do.astype(F32) * o.astype(F32)
    for j in range(HEADS):
        delta_ref[0, j : j + 1, :] = jnp.sum(prod[j * HEAD : (j + 1) * HEAD], axis=0, keepdims=True)

    @pl.when(step == last)
    def _():
        to_flat(aout, gout_ref, D, D)
        to_flat(agu, ggu_ref, D, 2 * FF)
        to_flat(adown, gdown_ref, FF, D)


def backward_kernel(
    me_ref, xt_ref, qkv_ref, do_ref, lse_ref, delta_ref, dr_ref, w_ref, gain_ref, cos_ref, sin_ref,
    gin_ref, gqkv_ref, gg_ref,
    krow, vrow, grads, acc,
):
    slices, _, span, _ = gin_ref.shape
    length = slices * span
    me = me_ref[0]

    clear(acc, 64)
    gg_ref[...] = jnp.zeros_like(gg_ref)
    clear(grads, 64)

    @pl.loop(0, length, step=TILE)
    def _(start):
        tok = pl.ds(pl.multiple_of(start, TILE), TILE)
        for j in range(KV_HEADS):
            krow[j, tok, :] = unflip(qkv_ref[0, KV0 + j * HEAD : KV0 + (j + 1) * HEAD, tok])
            vrow[j, tok, :] = unflip(qkv_ref[0, V0 + j * HEAD : V0 + (j + 1) * HEAD, tok])

    keep = tri_mask(TILE)

    def head(h, carry):
        kv = h // (HEADS // KV_HEADS)
        rows = pl.ds(pl.multiple_of(h * HEAD, HEAD), HEAD)
        krows = pl.ds(pl.multiple_of(KV0 + kv * HEAD, HEAD), HEAD)
        vrows = pl.ds(pl.multiple_of(V0 + kv * HEAD, HEAD), HEAD)
        for t in range(0, length, TILE):
            cols = slice(t, t + TILE)
            q = qkv_ref[0, rows, cols]
            do = do_ref[0, rows, cols]
            lse = lse_ref[0, pl.ds(h, 1), cols]
            delta = delta_ref[0, pl.ds(h, 1), cols]
            p = jnp.where(keep, jnp.exp(nn(krow[kv, cols, :], q) - lse), 0.0)
            ds = (p * (nn(vrow[kv, cols, :], do) - delta)).astype(BF)
            grads[vrows, cols] += nt(do, p.astype(BF))
            grads[krows, cols] += nt(q, ds)
            dq = nn(qkv_ref[0, krows, cols], ds)
            if t:
                p = jnp.exp(nn(krow[kv, 0:t, :], q) - lse)
                ds = (p * (nn(vrow[kv, 0:t, :], do) - delta)).astype(BF)
                grads[vrows, 0:t] += nt(do, p.astype(BF))
                grads[krows, 0:t] += nt(q, ds)
                dq = dq + nn(qkv_ref[0, krows, 0:t], ds)
            grads[rows, cols] = dq * 0.125
        return carry

    lax.fori_loop(0, HEADS, head, 0)

    gain = gain_ref[...]

    @pl.loop(0, slices)
    def _(k):
        at = pl.multiple_of((me ^ k) * span, span)
        cols = pl.ds(at, span)
        cos = cos_ref[:, cols]
        sin = sin_ref[:, cols]
        parts = []
        for j in range(HEADS + KV_HEADS):
            g1 = grads[j * HEAD : j * HEAD + HALF, cols]
            g2 = grads[j * HEAD + HALF : (j + 1) * HEAD, cols]
            parts.append((g1 * cos + g2 * sin).astype(BF))
            parts.append((g2 * cos - g1 * sin).astype(BF))
        parts.append(grads[V0:, cols].astype(BF))
        dp = jnp.concatenate(parts, axis=0)
        x = xt_ref[0, :, cols].astype(F32)
        inv = inverse_rms(x)
        n = x * inv
        normed = (n * gain).astype(BF)
        add_chunks(acc, nt(normed, dp))
        dh = nn(w_ref[...], dp)
        dhn = dh * n
        part = dhn[:, 0:128]
        for c in range(128, span, 128):
            part = part + dhn[:, c : c + 128]
        gg_ref[...] += part
        e = dh * gain
        gin = dr_ref[0, :, cols] + inv * (e - n * (jnp.sum(e * n, axis=0, keepdims=True) * (1.0 / D)))
        gin_ref[k, 0] = unflip(gin.astype(BF))

    to_flat(acc, gqkv_ref, D, QKVW)


WHOLE = pl.BlockSpec(memory_space=pltpu.VMEM)


def attention_forward(me, x_parts, wt, gain, cos, sin):
    slices = len(x_parts)
    seqs, span, _ = x_parts[0].shape
    length = slices * span
    by_seq = lambda rows: pl.BlockSpec((1, rows, length), lambda s, me: (s, 0, 0))
    return pl.pallas_call(
        functools.partial(forward_kernel, slices),
        grid_spec=pltpu.PrefetchScalarGridSpec(
            num_scalar_prefetch=1,
            grid=(seqs,),
            in_specs=[
                *[pl.BlockSpec((1, span, D), lambda s, me: (s, 0, 0))] * slices,
                WHOLE, WHOLE, WHOLE, WHOLE,
            ],
            out_specs=[by_seq(D), by_seq(QKVW), by_seq(D), by_seq(HEADS)],
            scratch_shapes=[pltpu.VMEM((KV_HEADS, length, HEAD), BF)],
        ),
        out_shape=[
            jax.ShapeDtypeStruct((seqs, D, length), BF),
            jax.ShapeDtypeStruct((seqs, QKVW, length), BF),
            jax.ShapeDtypeStruct((seqs, D, length), BF),
            jax.ShapeDtypeStruct((seqs, HEADS, length), F32),
        ],
        compiler_params=pltpu.CompilerParams(vmem_limit_bytes=48 << 20),
        cost_estimate=pl.CostEstimate(
            flops=seqs * (2 * length * D * QKVW + 6 * HEADS * length * length * HEAD),
            bytes_accessed=seqs * length * 7000,
            transcendentals=seqs * HEADS * length * length // 2,
        ),
        name="attention_forward",
    )(me, *x_parts, wt, gain, cos, sin)


def middle(me, xt, o, dy_stack, wo, wgu, wd, gain):
    slices, seqs, span, _ = dy_stack.shape
    length = slices * span
    tile = lambda rows: pl.BlockSpec((1, rows, span), lambda s, k, me: (s, 0, k ^ me[0]))
    stacked = pl.BlockSpec((1, 1, span, D), lambda s, k, me: (k, s, 0, 0))
    return pl.pallas_call(
        middle_kernel,
        grid_spec=pltpu.PrefetchScalarGridSpec(
            num_scalar_prefetch=1,
            grid=(seqs, slices),
            in_specs=[tile(D), tile(D), stacked, WHOLE, WHOLE, WHOLE, WHOLE],
            out_specs=[stacked, tile(D), tile(D), tile(HEADS), WHOLE, WHOLE, WHOLE, WHOLE],
            scratch_shapes=[
                pltpu.VMEM((D, D), BF),
                pltpu.VMEM((D, 2 * FF), BF),
                pltpu.VMEM((FF, D), BF),
                pltpu.VMEM((D, D), BF),
                pltpu.VMEM((2 * FF, D), BF),
                pltpu.VMEM((D, FF), BF),
                pltpu.VMEM((5, D, 128), F32),
                pltpu.VMEM((D, 2 * FF), F32),
                pltpu.VMEM((5, FF, 128), F32),
            ],
        ),
        out_shape=[
            jax.ShapeDtypeStruct((slices, seqs, span, D), BF),
            jax.ShapeDtypeStruct((seqs, D, length), F32),
            jax.ShapeDtypeStruct((seqs, D, length), BF),
            jax.ShapeDtypeStruct((seqs, HEADS, length), F32),
            jax.ShapeDtypeStruct((D * D // 128, 128), F32),
            jax.ShapeDtypeStruct((D * 2 * FF // 128, 128), F32),
            jax.ShapeDtypeStruct((FF * D // 128, 128), F32),
            jax.ShapeDtypeStruct((D, 128), F32),
        ],
        compiler_params=pltpu.CompilerParams(vmem_limit_bytes=60 << 20),
        cost_estimate=pl.CostEstimate(
            flops=seqs * length * 6 * (D * D + 3 * D * FF),
            bytes_accessed=seqs * length * 8000 + 12000000,
            transcendentals=seqs * length * FF,
        ),
        name="middle",
    )(me, xt, o, dy_stack, wo, wgu, wd, gain)


def attention_backward(seq, me, xt, qkv, do, lse, delta, dr, w, gain, cos, sin, slices):
    _, _, length = xt.shape
    span = length // slices
    by_seq = lambda rows: pl.BlockSpec((1, rows, length), lambda s, me: (seq, 0, 0))
    return pl.pallas_call(
        backward_kernel,
        grid_spec=pltpu.PrefetchScalarGridSpec(
            num_scalar_prefetch=1,
            grid=(1,),
            in_specs=[
                by_seq(D), by_seq(QKVW), by_seq(D), by_seq(HEADS), by_seq(HEADS), by_seq(D),
                WHOLE, WHOLE, WHOLE, WHOLE,
            ],
            out_specs=[
                pl.BlockSpec((slices, 1, span, D), lambda s, me: (0, 0, 0, 0)),
                WHOLE, WHOLE,
            ],
            scratch_shapes=[
                pltpu.VMEM((KV_HEADS, length, HEAD), BF),
                pltpu.VMEM((KV_HEADS, length, HEAD), BF),
                pltpu.VMEM((QKVW, length), F32),
                pltpu.VMEM((8, D, 128), F32),
            ],
        ),
        out_shape=[
            jax.ShapeDtypeStruct((slices, 1, span, D), BF),
            jax.ShapeDtypeStruct((D * QKVW // 128, 128), F32),
            jax.ShapeDtypeStruct((D, 128), F32),
        ],
        compiler_params=pltpu.CompilerParams(vmem_limit_bytes=56 << 20),
        cost_estimate=pl.CostEstimate(
            flops=4 * length * D * QKVW + 10 * HEADS * length * length * HEAD,
            bytes_accessed=length * 9000,
            transcendentals=HEADS * length * length // 2,
        ),
        name="attention_backward",
    )(me, xt, qkv, do, lse, delta, dr, w, gain, cos, sin)


def place_kernel(me_ref, *refs):
    parts, out_ref, sems = refs[:-2], refs[-2], refs[-1]
    copies = [
        pltpu.make_async_copy(part, out_ref.at[me_ref[0] ^ k], sems.at[k]) for k, part in enumerate(parts)
    ]
    for copy in copies:
        copy.start()
    for copy in copies:
        copy.wait()


def place(me, parts):
    any_space = pl.BlockSpec(memory_space=pl.ANY)
    return pl.pallas_call(
        place_kernel,
        grid_spec=pltpu.PrefetchScalarGridSpec(
            num_scalar_prefetch=1,
            grid=(1,),
            in_specs=[any_space] * len(parts),
            out_specs=any_space,
            scratch_shapes=[pltpu.SemaphoreType.DMA((len(parts),))],
        ),
        out_shape=jax.ShapeDtypeStruct((len(parts),) + parts[0].shape, parts[0].dtype),
        cost_estimate=pl.CostEstimate(flops=0, bytes_accessed=4 * len(parts) * parts[0].size, transcendentals=0),
        name="place",
    )(me, *parts)


def partner(array, name, bits):
    return lax.ppermute(array, name, [(i, i ^ bits) for i in range(lax.axis_size(name))])


def digit_of(name, stride, count):
    return (lax.axis_index(name) // stride) % count


def gather_digit(array, name, stride, count):
    parts = [array] + [partner(array, name, k * stride) for k in range(1, count)]
    digit = digit_of(name, stride, count)
    bit = 1
    while bit < count:
        swap = (digit & bit) != 0
        parts = [jnp.where(swap, parts[k ^ bit], parts[k]) for k in range(count)]
        bit *= 2
    return jnp.stack(parts)


def sum_digit(terms, axis, name, stride, count, dtype):
    digit = digit_of(name, stride, count)
    total = lax.dynamic_index_in_dim(terms, digit, axis, keepdims=False).astype(F32)
    for k in range(1, count):
        piece = lax.dynamic_index_in_dim(terms, digit ^ k, axis, keepdims=False).astype(BF)
        total = total + partner(piece, name, k * stride).astype(F32)
    return total.astype(dtype)


def local(tokens, w_qkv, w_out, w_gate_up, w_down, gains, cotangent):
    both = ("dp", "ctx")
    slices = lax.axis_size("ctx")
    across = lax.axis_size("dp")
    world = slices * across
    span = tokens.shape[1]
    seqs = tokens.shape[0] // slices
    length = slices * span
    ctx = lax.axis_index("ctx")
    me = ctx.astype(jnp.int32).reshape(1)
    nz = min(4, across)
    nx = across // nz
    core = ("ctx", 1, 2)
    y = ("ctx", 2, slices // 2)
    x = ("dp", 1, nx)
    z = ("dp", nx, nz)

    def exchange(array):
        grouped = array.reshape(slices, seqs, span, D)
        parts = [lax.dynamic_index_in_dim(grouped, ctx ^ k, 0, keepdims=False) for k in range(slices)]
        return parts[:1] + [partner(parts[k], "ctx", k) for k in range(1, slices)]

    def give_back(parts):
        return parts[:1] + [partner(parts[k], "ctx", k) for k in range(1, slices)]

    def reduce_terms(flat, order):
        terms = flat.reshape(nz, nx, slices // 2, 2, -1, 128)
        terms = sum_digit(terms, 3, *core, BF)
        if order == "xy":
            terms = sum_digit(terms, 1, *x, BF)
            terms = sum_digit(terms, 1, *y, BF)
        else:
            terms = sum_digit(terms, 2, *y, BF)
            terms = sum_digit(terms, 1, *x, BF)
        return sum_digit(terms, 0, *z, F32).reshape(-1)

    def shares(flat):
        rows = flat.reshape(world, -1)
        return jnp.pad(rows, ((0, 0), (0, -rows.shape[1] % 128)))

    n_qkv = w_qkv.shape[0]
    n_gain = gains.shape[0]
    early = jnp.concatenate([w_qkv, gains])
    early = jnp.pad(early, (0, -early.shape[0] % 1024)).reshape(-1, 128)
    for digit in (y, z, x, core):
        early = gather_digit(early, *digit)
    early = early.reshape(2, nx, nz, slices // 2, -1).transpose(2, 1, 3, 0, 4).reshape(world, -1)
    mat_qkv = early[:, :n_qkv].reshape(D, QKVW)
    gain_all = early[:, n_qkv : n_qkv + n_gain].reshape(2, D, 1).astype(F32)
    x_parts = exchange(tokens)
    rest = lax.all_gather(jnp.concatenate([w_gate_up, w_down, w_out]), both, axis=0, tiled=False)
    c1 = w_gate_up.shape[0]
    c2 = c1 + w_down.shape[0]
    flat_gu = rest[:, :c1].reshape(-1, 128)
    flat_down = rest[:, c1:c2].reshape(-1, 128)
    flat_out = rest[:, c2:].reshape(-1, 128)
    cos, sin = rotary_tables(length)
    xt, qkv, o, lse = attention_forward(me, x_parts, mat_qkv.T, gain_all[0], cos, sin)
    dy_stack = jnp.stack(exchange(cotangent))
    out_stack, dr, do, delta, g_out, g_gu, g_down, gg2 = middle(
        me, xt, o, dy_stack, flat_out, flat_gu, flat_down, gain_all[1]
    )
    output = place(me, give_back([out_stack[k] for k in range(slices)])).reshape(tokens.shape)
    own_gu = reduce_terms(shares(g_gu), "xy")
    own_down = reduce_terms(shares(g_down), "yx")
    own_out = reduce_terms(shares(g_out), "yx")
    back = [
        attention_backward(s, me, xt, qkv, do, lse, delta, dr, mat_qkv, gain_all[0], cos, sin, slices)
        for s in range(seqs)
    ]
    returned = [give_back([b[0][k] for k in range(slices)]) for b in back]
    grad_input = jnp.concatenate([place(me, parts) for parts in returned], axis=1).reshape(tokens.shape)
    g_qkv = sum(b[1] for b in back)
    gg = jnp.concatenate([jnp.sum(sum(b[2] for b in back), axis=1), jnp.sum(gg2, axis=1)])
    late = jnp.concatenate([g_qkv.reshape(world, -1), gg.reshape(world, -1)], axis=1)
    own_late = reduce_terms(shares(late), "xy")
    return (
        output,
        grad_input,
        own_late[:n_qkv],
        own_out[: w_out.shape[0]],
        own_gu[:c1],
        own_down[: w_down.shape[0]],
        own_late[n_qkv : n_qkv + n_gain],
    )


def solution(mesh):
    flat = P(("dp", "ctx"))
    rows = P("dp", "ctx", None)
    return jax.shard_map(
        local,
        mesh=mesh,
        in_specs=(rows, flat, flat, flat, flat, flat, rows),
        out_specs=(rows, rows, flat, flat, flat, flat, flat),
        check_vma=False,
    )
```

```python
import functools
import math

import jax
import jax.numpy as jnp
from jax import lax
from jax.experimental import pallas as pl
from jax.experimental.pallas import tpu as pltpu
from jax.sharding import PartitionSpec as P

D = 576
HEADS = 9
KV_HEADS = 3
HEAD = 64
GROUP = HEADS // KV_HEADS
FF = 1536
QKVW = 960
KV0 = D
V0 = D + KV_HEADS * HEAD
HALF = HEAD // 2
TILE = 256

EPSILON = 1e-05
THETA_BASE = 100000.0
NEG_FILL = -1e30
BF = jnp.bfloat16
F32 = jnp.float32


def nn(a, b):
    return lax.dot_general(a, b, (((1,), (0,)), ((), ())), preferred_element_type=F32)


def nt(a, b):
    return lax.dot_general(a, b, (((1,), (1,)), ((), ())), preferred_element_type=F32)


def eye(size):
    r = lax.broadcasted_iota(jnp.int32, (size, size), 0)
    c = lax.broadcasted_iota(jnp.int32, (size, size), 1)
    return jnp.where(r == c, 1.0, 0.0).astype(BF)


def col_chunks(width, step=128):
    return [(c, min(step, width - c)) for c in range(0, width, step)]


def unflip(cols):
    return nt(eye(cols.shape[1]), cols).astype(BF)


def inverse_rms(cols):
    return lax.rsqrt(jnp.sum(cols * cols, axis=0, keepdims=True) * (1.0 / D) + EPSILON)


def rotary_tables(length):
    halves = jnp.arange(0, HEAD, 2).astype(F32) / HEAD
    inverse = jnp.exp(-math.log(THETA_BASE) * halves)
    angles = inverse[:, None] * jnp.arange(length).astype(F32)[None, :]
    return jnp.cos(angles), jnp.sin(angles)


def tri_mask(size):
    key = lax.broadcasted_iota(jnp.int32, (size, size), 0)
    query = lax.broadcasted_iota(jnp.int32, (size, size), 1)
    return key <= query


def lane_low(size):
    return lax.broadcasted_iota(jnp.int32, (size, 128), 1) < 64


def to_flat(rows_ref, flat_ref, rows, width):
    if width % 128 == 0:
        n = width // 128

        @pl.loop(0, n)
        def _(c):
            flat_ref[pl.ds(c, rows, stride=n), :] = rows_ref[:, pl.ds(pl.multiple_of(c * 128, 128), 128)]

        return
    n = 2 * width // 128
    half = rows // 2
    low = lane_low(half)
    even = lambda c: rows_ref[c, pl.ds(0, half, stride=2), :]
    odd = lambda c: pltpu.roll(rows_ref[c, pl.ds(1, half, stride=2), :], 64, 1)
    for c in range(n // 2):
        flat_ref[pl.ds(c, half, stride=n), :] = even(c)
    before = odd(0)
    flat_ref[pl.ds(n // 2, half, stride=n), :] = jnp.where(low, even(n // 2), before)
    for c in range(n // 2):
        after = odd(c + 1)
        flat_ref[pl.ds(n // 2 + 1 + c, half, stride=n), :] = jnp.where(low, before, after)
        before = after


def from_flat(flat_ref, rows_ref, rows, width):
    if width % 128 == 0:
        n = width // 128

        @pl.loop(0, n)
        def _(c):
            rows_ref[:, pl.ds(pl.multiple_of(c * 128, 128), 128)] = flat_ref[
                pl.ds(c, rows, stride=n), :
            ].astype(rows_ref.dtype)

        return
    n = 2 * width // 128
    half = rows // 2
    low = lane_low(half)
    take = lambda c: flat_ref[pl.ds(c, half, stride=n), :]
    for c in range(n // 2 + 1):
        rows_ref[c, pl.ds(0, half, stride=2), :] = take(c)
    before = pltpu.roll(take(n // 2), 64, 1)
    for c in range(n // 2):
        after = pltpu.roll(take(n // 2 + 1 + c), 64, 1)
        rows_ref[c, pl.ds(1, half, stride=2), :] = jnp.where(low, before, after)
        before = after
    rows_ref[n // 2, pl.ds(1, half, stride=2), :] = before


def convert(src_ref, dst_ref, rows, step):
    @pl.loop(0, rows, step=step)
    def _(i):
        at = pl.ds(pl.multiple_of(i, step), step)
        dst_ref[at, :] = src_ref[at, 0 : dst_ref.shape[1]].astype(dst_ref.dtype)


def clear(ref, step):
    @pl.loop(0, ref.shape[-2], step=step)
    def _(i):
        at = pl.ds(pl.multiple_of(i, step), step)
        if len(ref.shape) == 3:
            ref[:, at, :] = jnp.zeros((ref.shape[0], step, ref.shape[2]), ref.dtype)
        else:
            ref[at, :] = jnp.zeros((step, ref.shape[1]), ref.dtype)


def add_chunks(ref, value):
    for c, w in col_chunks(value.shape[1]):
        ref[c // 128, :, 0:w] += value[:, c : c + w]


def join_chunks(src_ref, dst_ref):
    for c, w in col_chunks(dst_ref.shape[1]):
        dst_ref[:, c : c + w] = src_ref[c // 128, :, 0:w].astype(dst_ref.dtype)


def prepare_kernel(flat_ref, w_ref, wt_ref, flat, rows):
    convert(flat_ref, flat, flat.shape[0], 240)
    from_flat(flat, rows, D, QKVW)
    join_chunks(rows, w_ref)
    for c, w in col_chunks(QKVW):
        wt_ref[c : c + w, :] = nt(eye(w), w_ref[:, c : c + w]).astype(BF)


def forward_kernel(slices, me_ref, *refs):
    x_refs = refs[:slices]
    wt_ref, gain_ref, cos_ref, sin_ref = refs[slices : slices + 4]
    xt_ref, qkv_ref, o_ref, lse_ref, krow = refs[-5:]
    _, _, span = x_refs[0].shape
    length = slices * span
    me = me_ref[0]
    for k in range(slices):
        at = pl.multiple_of((me ^ k) * span, span)
        xt_ref[0, :, pl.ds(at, span)] = x_refs[k][0]
    gain = gain_ref[...]

    @pl.loop(0, length, step=TILE)
    def _(start):
        tok = pl.ds(pl.multiple_of(start, TILE), TILE)
        x = xt_ref[0, :, tok].astype(F32)
        normed = (x * inverse_rms(x) * gain).astype(BF)
        proj = nn(wt_ref[...], normed)
        cos = cos_ref[:, tok]
        sin = sin_ref[:, tok]
        for j in range(HEADS + KV_HEADS):
            u1 = proj[j * HEAD : j * HEAD + HALF]
            u2 = proj[j * HEAD + HALF : (j + 1) * HEAD]
            r1 = (u1 * cos - u2 * sin).astype(BF)
            r2 = (u2 * cos + u1 * sin).astype(BF)
            if j < HEADS:
                r1 = r1 * jnp.asarray(0.125, BF)
                r2 = r2 * jnp.asarray(0.125, BF)
            qkv_ref[0, j * HEAD : j * HEAD + HALF, tok] = r1
            qkv_ref[0, j * HEAD + HALF : (j + 1) * HEAD, tok] = r2
        qkv_ref[0, V0:, tok] = proj[V0:].astype(BF)
        for j in range(KV_HEADS):
            krow[j, tok, :] = unflip(qkv_ref[0, KV0 + j * HEAD : KV0 + (j + 1) * HEAD, tok])

    keep = tri_mask(TILE)

    def head(h, carry):
        kv = h // GROUP
        rows = pl.ds(pl.multiple_of(h * HEAD, HEAD), HEAD)
        vrows = pl.ds(pl.multiple_of(V0 + kv * HEAD, HEAD), HEAD)
        for t in range(0, length, TILE):
            cols = slice(t, t + TILE)
            q = qkv_ref[0, rows, cols]
            last = jnp.where(keep, nn(krow[kv, cols, :], q), NEG_FILL)
            top = jnp.max(last, axis=0, keepdims=True)
            if t:
                before = nn(krow[kv, 0:t, :], q)
                top = jnp.maximum(top, jnp.max(before, axis=0, keepdims=True))
            e = jnp.exp(last - top)
            total = jnp.sum(e, axis=0, keepdims=True)
            acc = nn(qkv_ref[0, vrows, cols], e.astype(BF))
            if t:
                e = jnp.exp(before - top)
                total = total + jnp.sum(e, axis=0, keepdims=True)
                acc = acc + nn(qkv_ref[0, vrows, 0:t], e.astype(BF))
            o_ref[0, rows, cols] = (acc * (1.0 / total)).astype(BF)
            lse_ref[0, kv, pl.ds(h % GROUP, 1), cols] = top + jnp.log(total)
        return carry

    lax.fori_loop(0, HEADS, head, 0)


def middle_kernel(
    me_ref, xt_ref, o_ref, dy_ref, fo_ref, fgu_ref, fd_ref, gain_ref,
    out_ref, dr_ref, do_ref, delta_ref, gout_ref, ggu_ref, gdown_ref, gg_ref,
    wo_ref, wgu_ref, wd_ref, wot, wgut, wdt, aout, agu, adown,
):
    step = pl.program_id(0) * pl.num_programs(1) + pl.program_id(1)
    last = pl.num_programs(0) * pl.num_programs(1) - 1

    @pl.when(step == 0)
    def _():
        convert(fgu_ref, ggu_ref, fgu_ref.shape[0], 256)
        from_flat(ggu_ref, wgu_ref, D, 2 * FF)
        convert(fd_ref, gdown_ref, fd_ref.shape[0], 256)
        from_flat(gdown_ref, adown, FF, D)
        join_chunks(adown, wd_ref)
        convert(fo_ref, gout_ref, fo_ref.shape[0], 96)
        from_flat(gout_ref, aout, D, D)
        join_chunks(aout, wo_ref)

        @pl.loop(0, 2 * FF, step=TILE)
        def _(c):
            at = pl.ds(pl.multiple_of(c, TILE), TILE)
            wgut[at, :] = nt(eye(TILE), wgu_ref[:, at]).astype(BF)

        for c, w in col_chunks(D):
            wdt[c : c + w, :] = nt(eye(w), wd_ref[:, c : c + w]).astype(BF)
            wot[c : c + w, :] = nt(eye(w), wo_ref[:, c : c + w]).astype(BF)
        clear(aout, 64)
        clear(agu, 16)
        clear(adown, 64)
        gg_ref[...] = jnp.zeros_like(gg_ref)

    gain = gain_ref[...]
    o = o_ref[0]
    r = xt_ref[0].astype(F32) + nn(wot[...], o)
    inv = inverse_rms(r)
    n = r * inv
    h = (n * gain).astype(BF)
    a = nn(wgut[0:FF, :], h)
    u = nn(wgut[FF:, :], h)
    sg = 1.0 / (1.0 + jnp.exp(-a))
    act = a * sg
    m = (act * u).astype(BF)
    out_ref[0, 0] = (r + nn(wdt[...], m)).astype(BF)
    dyt = dy_ref[0, 0]
    add_chunks(adown, nt(m, dyt))
    dm = nn(wd_ref[...], dyt)
    da = (dm * u * sg * (1.0 + a * (1.0 - sg))).astype(BF)
    du = (dm * act).astype(BF)
    agu[:, 0:FF] += nt(h, da)
    agu[:, FF:] += nt(h, du)
    dh = nn(wgu_ref[:, 0:FF], da) + nn(wgu_ref[:, FF:], du)
    dhn = dh * n
    part = dhn[:, 0:128]
    for c in range(128, dhn.shape[1], 128):
        part = part + dhn[:, c : c + 128]
    gg_ref[...] += part
    e = dh * gain
    dr = dyt.astype(F32) + inv * (e - n * (jnp.sum(e * n, axis=0, keepdims=True) * (1.0 / D)))
    dr_ref[0] = dr
    db = dr.astype(BF)
    add_chunks(aout, nt(o, db))
    do = nn(wo_ref[...], db).astype(BF)
    do_ref[0] = do
    prod = do.astype(F32) * o.astype(F32)
    for j in range(HEADS):
        delta_ref[0, j // GROUP, j % GROUP : j % GROUP + 1, :] = jnp.sum(prod[j * HEAD : (j + 1) * HEAD], axis=0, keepdims=True)

    @pl.when(step == last)
    def _():
        to_flat(aout, gout_ref, D, D)
        to_flat(agu, ggu_ref, D, 2 * FF)
        to_flat(adown, gdown_ref, FF, D)


def attend_back_kernel(
    me_ref, q_ref, k_ref, v_ref, do_ref, lse_ref, delta_ref, cos_ref, sin_ref, dp_ref, krow, vrow, grads
):
    length = q_ref.shape[2]
    k0 = GROUP * HEAD
    v0 = k0 + HEAD
    clear(grads, 64)

    @pl.loop(0, length, step=TILE)
    def _(start):
        tok = pl.ds(pl.multiple_of(start, TILE), TILE)
        krow[tok, :] = unflip(k_ref[0, :, tok])
        vrow[tok, :] = unflip(v_ref[0, :, tok])

    keep = tri_mask(TILE)

    def head(h, carry):
        rows = pl.ds(pl.multiple_of(h * HEAD, HEAD), HEAD)
        for t in range(0, length, TILE):
            cols = slice(t, t + TILE)
            q = q_ref[0, rows, cols]
            do = do_ref[0, rows, cols]
            lse = lse_ref[0, 0, pl.ds(h, 1), cols]
            delta = delta_ref[0, 0, pl.ds(h, 1), cols]
            p = jnp.where(keep, jnp.exp(nn(krow[cols, :], q) - lse), 0.0)
            ds = (p * (nn(vrow[cols, :], do) - delta)).astype(BF)
            grads[v0:, cols] += nt(do, p.astype(BF))
            grads[k0:v0, cols] += nt(q, ds)
            dq = nn(k_ref[0, :, cols], ds)
            if t:
                p = jnp.exp(nn(krow[0:t, :], q) - lse)
                ds = (p * (nn(vrow[0:t, :], do) - delta)).astype(BF)
                grads[v0:, 0:t] += nt(do, p.astype(BF))
                grads[k0:v0, 0:t] += nt(q, ds)
                dq = dq + nn(k_ref[0, :, 0:t], ds)
            grads[rows, cols] = dq * 0.125
        return carry

    lax.fori_loop(0, GROUP, head, 0)

    @pl.loop(0, length, step=TILE)
    def _(start):
        tok = pl.ds(pl.multiple_of(start, TILE), TILE)
        cos = cos_ref[:, tok]
        sin = sin_ref[:, tok]
        for j in range(GROUP + 1):
            one = slice(j * HEAD, j * HEAD + HALF)
            two = slice(j * HEAD + HALF, (j + 1) * HEAD)
            g1 = grads[one, tok]
            g2 = grads[two, tok]
            dp_ref[0, one, tok] = (g1 * cos + g2 * sin).astype(BF)
            dp_ref[0, two, tok] = (g2 * cos - g1 * sin).astype(BF)
        dp_ref[0, v0:, tok] = grads[v0:, tok].astype(BF)


def project_back_kernel(me_ref, d0_ref, d1_ref, d2_ref, xt_ref, dr_ref, w_ref, gain_ref, *refs):
    gin_ref, gqkv_ref, gg_ref, acc = refs[-4:]

    @pl.when(pl.program_id(0) == 0)
    def _():
        if len(refs) > 4:
            from_flat(refs[0], acc, D, QKVW)
            gg_ref[...] = refs[1][...]
        else:
            clear(acc, 64)
            gg_ref[...] = jnp.zeros_like(gg_ref)

    groups = (d0_ref, d1_ref, d2_ref)
    k0 = GROUP * HEAD
    v0 = k0 + HEAD
    dp = jnp.concatenate(
        [g[0, 0:k0, :] for g in groups] + [g[0, k0:v0, :] for g in groups] + [g[0, v0:, :] for g in groups], axis=0
    )
    x = xt_ref[0].astype(F32)
    inv = inverse_rms(x)
    n = x * inv
    gain = gain_ref[...]
    add_chunks(acc, nt((n * gain).astype(BF), dp))
    dh = nn(w_ref[...], dp)
    dhn = dh * n
    part = dhn[:, 0:128]
    for c in range(128, dhn.shape[1], 128):
        part = part + dhn[:, c : c + 128]
    gg_ref[...] += part
    e = dh * gain
    gin = dr_ref[0] + inv * (e - n * (jnp.sum(e * n, axis=0, keepdims=True) * (1.0 / D)))
    gin_ref[0] = gin.astype(BF)

    @pl.when(pl.program_id(0) == pl.num_programs(0) - 1)
    def _():
        to_flat(acc, gqkv_ref, D, QKVW)


WHOLE = pl.BlockSpec(memory_space=pltpu.VMEM)


def prepare(flat):
    return pl.pallas_call(
        prepare_kernel,
        in_specs=[WHOLE],
        out_specs=[WHOLE, WHOLE],
        out_shape=[jax.ShapeDtypeStruct((D, QKVW), BF), jax.ShapeDtypeStruct((QKVW, D), BF)],
        scratch_shapes=[pltpu.VMEM(flat.shape, F32), pltpu.VMEM((8, D, 128), F32)],
        compiler_params=pltpu.CompilerParams(vmem_limit_bytes=24 << 20),
        cost_estimate=pl.CostEstimate(flops=2 * D * D * QKVW, bytes_accessed=6 * D * QKVW, transcendentals=0),
        name="prepare",
    )(flat)


def attention_forward(seq, me, x_parts, wt, gain, cos, sin, before):
    slices = len(x_parts)
    seqs, _, span = x_parts[0].shape
    length = slices * span
    by_seq = lambda rows: pl.BlockSpec((1, rows, length), lambda s, me: (seq, 0, 0))
    stats = pl.BlockSpec((1, KV_HEADS, GROUP, length), lambda s, me: (seq, 0, 0, 0))
    n_in = 1 + slices + 4
    return pl.pallas_call(
        functools.partial(forward_kernel, slices),
        grid_spec=pltpu.PrefetchScalarGridSpec(
            num_scalar_prefetch=1,
            grid=(1,),
            in_specs=[
                *[pl.BlockSpec((1, D, span), lambda s, me: (seq, 0, 0))] * slices,
                WHOLE, WHOLE, WHOLE, WHOLE,
                *[pl.BlockSpec(memory_space=pl.ANY)] * len(before),
            ],
            out_specs=[by_seq(D), by_seq(QKVW), by_seq(D), stats],
            scratch_shapes=[pltpu.VMEM((KV_HEADS, length, HEAD), BF)],
        ),
        out_shape=[
            jax.ShapeDtypeStruct((seqs, D, length), BF),
            jax.ShapeDtypeStruct((seqs, QKVW, length), BF),
            jax.ShapeDtypeStruct((seqs, D, length), BF),
            jax.ShapeDtypeStruct((seqs, KV_HEADS, GROUP, length), F32),
        ],
        input_output_aliases={n_in + i: i for i in range(len(before))},
        compiler_params=pltpu.CompilerParams(vmem_limit_bytes=40 << 20),
        cost_estimate=pl.CostEstimate(
            flops=2 * length * D * QKVW + 16 * HEADS * length * length * HEAD,
            bytes_accessed=length * 7000,
            transcendentals=HEADS * length * length // 2,
        ),
        name="attention_forward",
    )(me, *x_parts, wt, gain, cos, sin, *before)


def middle(me, xt, o, dy_stack, wo, wgu, wd, gain):
    slices, seqs, _, span = dy_stack.shape
    length = slices * span
    stats = pl.BlockSpec((1, KV_HEADS, GROUP, span), lambda s, k, me: (s, 0, 0, k ^ me[0]))
    tile = lambda rows: pl.BlockSpec((1, rows, span), lambda s, k, me: (s, 0, k ^ me[0]))
    stacked = pl.BlockSpec((1, 1, D, span), lambda s, k, me: (k, s, 0, 0))
    return pl.pallas_call(
        middle_kernel,
        grid_spec=pltpu.PrefetchScalarGridSpec(
            num_scalar_prefetch=1,
            grid=(seqs, slices),
            in_specs=[tile(D), tile(D), stacked, WHOLE, WHOLE, WHOLE, WHOLE],
            out_specs=[stacked, tile(D), tile(D), stats, WHOLE, WHOLE, WHOLE, WHOLE],
            scratch_shapes=[
                pltpu.VMEM((D, D), BF),
                pltpu.VMEM((D, 2 * FF), BF),
                pltpu.VMEM((FF, D), BF),
                pltpu.VMEM((D, D), BF),
                pltpu.VMEM((2 * FF, D), BF),
                pltpu.VMEM((D, FF), BF),
                pltpu.VMEM((5, D, 128), F32),
                pltpu.VMEM((D, 2 * FF), F32),
                pltpu.VMEM((5, FF, 128), F32),
            ],
        ),
        out_shape=[
            jax.ShapeDtypeStruct((slices, seqs, D, span), BF),
            jax.ShapeDtypeStruct((seqs, D, length), F32),
            jax.ShapeDtypeStruct((seqs, D, length), BF),
            jax.ShapeDtypeStruct((seqs, KV_HEADS, GROUP, length), F32),
            jax.ShapeDtypeStruct((D * D // 128, 128), F32),
            jax.ShapeDtypeStruct((D * 2 * FF // 128, 128), F32),
            jax.ShapeDtypeStruct((FF * D // 128, 128), F32),
            jax.ShapeDtypeStruct((D, 128), F32),
        ],
        compiler_params=pltpu.CompilerParams(vmem_limit_bytes=60 << 20),
        cost_estimate=pl.CostEstimate(
            flops=seqs * length * 6 * (D * D + 3 * D * FF),
            bytes_accessed=seqs * length * 8000 + 12000000,
            transcendentals=seqs * length * FF,
        ),
        name="middle",
    )(me, xt, o, dy_stack, wo, wgu, wd, gain)


def attend_back(first, count, me, qkv, do, lse, delta, cos, sin):
    length = qkv.shape[2]
    width = (GROUP + 2) * HEAD
    at = lambda p: ((first + p) // KV_HEADS, (first + p) % KV_HEADS)
    rows = lambda n, base: pl.BlockSpec((1, n, length), lambda p, me: (at(p)[0], base + at(p)[1], 0))
    stats = pl.BlockSpec((1, 1, GROUP, length), lambda p, me: (*at(p), 0, 0))
    return pl.pallas_call(
        attend_back_kernel,
        grid_spec=pltpu.PrefetchScalarGridSpec(
            num_scalar_prefetch=1,
            grid=(count,),
            in_specs=[
                rows(GROUP * HEAD, 0), rows(HEAD, KV0 // HEAD), rows(HEAD, V0 // HEAD), rows(GROUP * HEAD, 0),
                stats, stats, WHOLE, WHOLE,
            ],
            out_specs=pl.BlockSpec((1, width, length), lambda p, me: (p, 0, 0)),
            scratch_shapes=[
                pltpu.VMEM((length, HEAD), BF),
                pltpu.VMEM((length, HEAD), BF),
                pltpu.VMEM((width, length), F32),
            ],
        ),
        out_shape=jax.ShapeDtypeStruct((count, width, length), BF),
        compiler_params=pltpu.CompilerParams(vmem_limit_bytes=40 << 20),
        cost_estimate=pl.CostEstimate(
            flops=count * 30 * GROUP * length * length * HEAD,
            bytes_accessed=count * length * 3000,
            transcendentals=count * GROUP * length * length // 2,
        ),
        name="attend_back",
    )(me, qkv, qkv, qkv, do, lse, delta, cos, sin)


def project_back(seq, me, pairs, xt, dr, w, gain, slices, earlier):
    length = xt.shape[2]
    span = length // slices
    width = (GROUP + 2) * HEAD
    tile = pl.BlockSpec((1, D, span), lambda k, me: (seq, 0, k ^ me[0]))
    return pl.pallas_call(
        project_back_kernel,
        grid_spec=pltpu.PrefetchScalarGridSpec(
            num_scalar_prefetch=1,
            grid=(slices,),
            in_specs=[
                *[pl.BlockSpec((1, width, span), lambda k, me, i=i: (i, 0, k ^ me[0])) for _, i in pairs],
                tile, tile, WHOLE, WHOLE, *[WHOLE] * len(earlier),
            ],
            out_specs=[pl.BlockSpec((1, D, span), lambda k, me: (k, 0, 0)), WHOLE, WHOLE],
            scratch_shapes=[pltpu.VMEM((8, D, 128), F32)],
        ),
        out_shape=[
            jax.ShapeDtypeStruct((slices, D, span), BF),
            jax.ShapeDtypeStruct((D * QKVW // 128, 128), F32),
            jax.ShapeDtypeStruct((D, 128), F32),
        ],
        compiler_params=pltpu.CompilerParams(vmem_limit_bytes=32 << 20),
        cost_estimate=pl.CostEstimate(
            flops=8 * length * D * QKVW, bytes_accessed=length * 8000 + 4000000, transcendentals=0
        ),
        name="project_back",
    )(me, *[array for array, _ in pairs], xt, dr, w, gain, *earlier)


def partner(array, name, bits):
    return lax.ppermute(array, name, [(i, i ^ bits) for i in range(lax.axis_size(name))])


def digit_of(name, stride, count):
    return (lax.axis_index(name) // stride) % count


def in_order(parts, digit):
    bit = 1
    while bit < len(parts):
        swap = (digit & bit) != 0
        parts = [jnp.where(swap, parts[k ^ bit], parts[k]) for k in range(len(parts))]
        bit *= 2
    return parts


def after(value, *others):
    others = [other for other in others if other is not None]
    return lax.optimization_barrier((value, *others))[0] if others else value


def gather_digit(array, name, stride, count, hold=None):
    parts = [array] + [after(partner(array, name, k * stride), hold) for k in range(1, count)]
    return jnp.stack(in_order(parts, digit_of(name, stride, count)))


def sum_digit(terms, axis, name, stride, count, dtype, hold=None):
    digit = digit_of(name, stride, count)
    total = lax.dynamic_index_in_dim(terms, digit, axis, keepdims=False).astype(F32)
    for k in range(1, count):
        piece = lax.dynamic_index_in_dim(terms, digit ^ k, axis, keepdims=False).astype(BF)
        total = total + after(partner(piece, name, k * stride), hold).astype(F32)
    return total.astype(dtype)


def local(tokens, w_qkv, w_out, w_gate_up, w_down, gains, cotangent):
    slices = lax.axis_size("ctx")
    across = lax.axis_size("dp")
    world = slices * across
    span = tokens.shape[1]
    seqs = tokens.shape[0] // slices
    length = slices * span
    ctx = lax.axis_index("ctx")
    me = ctx.astype(jnp.int32).reshape(1)
    nz = min(4, across)
    nx = across // nz
    ny = slices // 2
    core = ("ctx", 1, 2)
    y = ("ctx", 2, ny)
    x = ("dp", 1, nx)
    z = ("dp", nx, nz)

    def exchange(array, hold=None):
        grouped = array.transpose(0, 2, 1).reshape(slices, seqs, D, span)
        parts = [lax.dynamic_index_in_dim(grouped, ctx ^ k, 0, keepdims=False) for k in range(slices)]
        return parts[:1] + [after(partner(parts[k], "ctx", k), hold) for k in range(1, slices)]

    def give_back(stack, hold=None):
        parts = [stack[k] for k in range(slices)]
        parts = parts[:1] + [after(partner(parts[k], "ctx", k), hold) for k in range(1, slices)]
        return in_order(parts, ctx)

    def placed(stack):
        return stack.reshape(tokens.shape[0], D, span).transpose(0, 2, 1)

    def as_rows(shard):
        return jnp.pad(shard, (0, -shard.shape[0] % 1024)).reshape(-1, 128)

    def whole_flat(stack, order, size):
        stack = stack.transpose(*[order.index(d) for d in "zxyc"], 4, 5)
        return stack.reshape(world, -1, 128)[:, : -(-size // 128)].reshape(world, -1)[:, :size].reshape(-1, 128)

    def shares(flat):
        if flat.size % (world * 128) == 0:
            return flat.reshape(nz, nx, ny, 2, -1, 128)
        rows = flat.reshape(world, -1)
        return jnp.pad(rows, ((0, 0), (0, -rows.shape[1] % 128))).reshape(nz, nx, ny, 2, -1, 128)

    n_qkv = w_qkv.shape[0]
    n_gain = gains.shape[0]
    early = as_rows(jnp.concatenate([w_qkv, gains]))
    for digit in (y, x, z, core):
        early = gather_digit(early, *digit)
    early = early.transpose(1, 2, 3, 0, 4, 5).reshape(world, -1, 128)
    flat_qkv = early[:, : n_qkv // 128].reshape(-1, 128) if n_qkv % 128 == 0 else early.reshape(world, -1)[:, :n_qkv].reshape(-1, 128)
    gain_all = early.reshape(world, -1)[:, n_qkv : n_qkv + n_gain].reshape(2, D, 1).astype(F32)
    x_parts = exchange(tokens)
    down_rows = as_rows(w_down)
    gu1 = gather_digit(as_rows(w_gate_up), *z)
    both1 = gather_digit(jnp.concatenate([down_rows, as_rows(w_out)]), *z)
    gu2 = gather_digit(gu1, *y)
    both2 = gather_digit(both1, *x)
    cos, sin = rotary_tables(length)
    mat_qkv, mat_qkv_t = prepare(flat_qkv)
    forward = ()
    for s in range(seqs):
        order = after(me, gu2, both2) if s == 0 else after(me, gu3, both3)
        forward = attention_forward(s, order, x_parts, mat_qkv_t, gain_all[0], cos, sin, forward)
        if s == 0:
            gu3 = gather_digit(gu2, *x, forward[3])
            both3 = gather_digit(both2, *y, forward[3])
    xt, qkv, o, lse = forward
    flat_gu = whole_flat(gather_digit(gu3, *core, lse), "cxyz", w_gate_up.shape[0])
    both4 = gather_digit(both3, *core, lse)
    flat_down = whole_flat(both4[..., : down_rows.shape[0], :], "cyxz", w_down.shape[0])
    flat_out = whole_flat(both4[..., down_rows.shape[0] :, :], "cyxz", w_out.shape[0])
    dy_stack = jnp.stack(exchange(after(cotangent, gu2, both2), lse))
    out_stack, dr, do, delta, g_out, g_gu, g_down, gg2 = middle(
        me, xt, o, dy_stack, flat_out, flat_gu, flat_down, gain_all[1]
    )

    n_pairs = seqs * KV_HEADS
    pairs = []
    back = []
    sums = [shares(g) for g in (g_gu, g_down, g_out)]
    down_count = sums[1].shape[4]
    stages = [
        ((3, *core),) * 3,
        ((1, *x), (2, *y)),
        ((1, *y), (1, *x)),
    ]
    order = me

    def advance(hold):
        nonlocal sums
        if stages:
            sums = [sum_digit(r, *how, BF, hold) for r, how in zip(sums, stages.pop(0))]
            sums = [sums[0], jnp.concatenate(sums[1:], axis=-2)]
        return after(me, hold, *sums)

    for first in range(0, n_pairs, 2):
        count = min(2, n_pairs - first)
        dp = attend_back(first, count, order, qkv, do, lse, delta, cos, sin)
        if first == 0:
            out_stack = after(out_stack, dp)
        pairs += [(dp, i) for i in range(count)]
        if first == 0 or n_pairs - first <= 2 or len(pairs) < KV_HEADS * (len(back) + 1):
            order = advance(dp)
        while len(pairs) >= KV_HEADS * (len(back) + 1):
            s = len(back)
            back.append(
                project_back(
                    s, order, pairs[KV_HEADS * s : KV_HEADS * (s + 1)], xt, dr, mat_qkv, gain_all[0], slices,
                    back[-1][1:] if back else (),
                )
            )
            if len(back) < seqs:
                order = advance(back[-1][2])
    while stages:
        advance(None)
    own_gu, own_both = [sum_digit(r, 0, *z, F32, back[-1][2]) for r in sums]
    output = placed(jnp.stack(give_back(out_stack, back[-1][2])))
    returned = [jnp.stack(give_back(b[0], back[-1][2])) for b in back]
    grad_input = placed(jnp.stack(returned, axis=1))
    g_qkv, gg1 = back[-1][1:]
    gg = jnp.concatenate([jnp.sum(gg1, axis=1), jnp.sum(gg2, axis=1)])
    late = jnp.concatenate([g_qkv.reshape(world, -1), gg.reshape(world, -1)], axis=1)
    late = sum_digit(shares(late), 3, *core, BF)
    late = sum_digit(late, 1, *x, BF)
    late = sum_digit(late, 1, *y, BF)
    own_late = sum_digit(late, 0, *z, F32).reshape(-1)
    return (
        output,
        grad_input,
        own_late[:n_qkv],
        own_both[down_count:].reshape(-1)[: w_out.shape[0]],
        own_gu.reshape(-1)[: w_gate_up.shape[0]],
        own_both[:down_count].reshape(-1)[: w_down.shape[0]],
        own_late[n_qkv : n_qkv + n_gain],
    )


def solution(mesh):
    flat = P(("dp", "ctx"))
    rows = P("dp", "ctx", None)
    return jax.shard_map(
        local,
        mesh=mesh,
        in_specs=(rows, flat, flat, flat, flat, flat, rows),
        out_specs=(rows, rows, flat, flat, flat, flat, flat),
        check_vma=False,
    )
```

```python
import functools
import math

import jax
import jax.numpy as jnp
from jax import lax
from jax.experimental import pallas as pl
from jax.experimental.pallas import tpu as pltpu
from jax.sharding import PartitionSpec as P

D = 576
HEADS = 9
KV_HEADS = 3
HEAD = 64
GROUP = HEADS // KV_HEADS
FF = 1536
QKVW = 960
KV0 = D
V0 = D + KV_HEADS * HEAD
HALF = HEAD // 2
TILE = 256

EPSILON = 1e-05
THETA_BASE = 100000.0
NEG_FILL = -1e30
BF = jnp.bfloat16
F32 = jnp.float32


def nn(a, b):
    return lax.dot_general(a, b, (((1,), (0,)), ((), ())), preferred_element_type=F32)


def nt(a, b):
    return lax.dot_general(a, b, (((1,), (1,)), ((), ())), preferred_element_type=F32)


def eye(size):
    r = lax.broadcasted_iota(jnp.int32, (size, size), 0)
    c = lax.broadcasted_iota(jnp.int32, (size, size), 1)
    return jnp.where(r == c, 1.0, 0.0).astype(BF)


def col_chunks(width, step=128):
    return [(c, min(step, width - c)) for c in range(0, width, step)]


def unflip(cols):
    return nt(eye(cols.shape[1]), cols).astype(BF)


def inverse_rms(cols):
    return lax.rsqrt(jnp.sum(cols * cols, axis=0, keepdims=True) * (1.0 / D) + EPSILON)


def rotary_tables(length):
    halves = jnp.arange(0, HEAD, 2).astype(F32) / HEAD
    inverse = jnp.exp(-math.log(THETA_BASE) * halves)
    angles = inverse[:, None] * jnp.arange(length).astype(F32)[None, :]
    return jnp.cos(angles), jnp.sin(angles)


def tri_mask(size):
    key = lax.broadcasted_iota(jnp.int32, (size, size), 0)
    query = lax.broadcasted_iota(jnp.int32, (size, size), 1)
    return key <= query


def lane_low(size):
    return lax.broadcasted_iota(jnp.int32, (size, 128), 1) < 64


def to_flat(rows_ref, flat_ref, rows, width):
    if width % 128 == 0:
        n = width // 128

        @pl.loop(0, n)
        def _(c):
            flat_ref[pl.ds(c, rows, stride=n), :] = rows_ref[:, pl.ds(pl.multiple_of(c * 128, 128), 128)]

        return
    n = 2 * width // 128
    half = rows // 2
    low = lane_low(half)
    even = lambda c: rows_ref[c, pl.ds(0, half, stride=2), :]
    odd = lambda c: pltpu.roll(rows_ref[c, pl.ds(1, half, stride=2), :], 64, 1)
    for c in range(n // 2):
        flat_ref[pl.ds(c, half, stride=n), :] = even(c)
    before = odd(0)
    flat_ref[pl.ds(n // 2, half, stride=n), :] = jnp.where(low, even(n // 2), before)
    for c in range(n // 2):
        after = odd(c + 1)
        flat_ref[pl.ds(n // 2 + 1 + c, half, stride=n), :] = jnp.where(low, before, after)
        before = after


def from_flat(flat_ref, rows_ref, rows, width):
    if width % 128 == 0:
        n = width // 128

        @pl.loop(0, n)
        def _(c):
            rows_ref[:, pl.ds(pl.multiple_of(c * 128, 128), 128)] = flat_ref[
                pl.ds(c, rows, stride=n), :
            ].astype(rows_ref.dtype)

        return
    n = 2 * width // 128
    half = rows // 2
    low = lane_low(half)
    take = lambda c: flat_ref[pl.ds(c, half, stride=n), :]
    for c in range(n // 2 + 1):
        rows_ref[c, pl.ds(0, half, stride=2), :] = take(c)
    before = pltpu.roll(take(n // 2), 64, 1)
    for c in range(n // 2):
        after = pltpu.roll(take(n // 2 + 1 + c), 64, 1)
        rows_ref[c, pl.ds(1, half, stride=2), :] = jnp.where(low, before, after)
        before = after
    rows_ref[n // 2, pl.ds(1, half, stride=2), :] = before


def convert(src_ref, dst_ref, rows, step):
    @pl.loop(0, rows, step=step)
    def _(i):
        at = pl.ds(pl.multiple_of(i, step), step)
        dst_ref[at, :] = src_ref[at, 0 : dst_ref.shape[1]].astype(dst_ref.dtype)


def clear(ref, step):
    @pl.loop(0, ref.shape[-2], step=step)
    def _(i):
        at = pl.ds(pl.multiple_of(i, step), step)
        if len(ref.shape) == 3:
            ref[:, at, :] = jnp.zeros((ref.shape[0], step, ref.shape[2]), ref.dtype)
        else:
            ref[at, :] = jnp.zeros((step, ref.shape[1]), ref.dtype)


def add_chunks(ref, value):
    for c, w in col_chunks(value.shape[1]):
        ref[c // 128, :, 0:w] += value[:, c : c + w]


def join_chunks(src_ref, dst_ref):
    for c, w in col_chunks(dst_ref.shape[1]):
        dst_ref[:, c : c + w] = src_ref[c // 128, :, 0:w].astype(dst_ref.dtype)


def prepare_kernel(flat_ref, w_ref, wt_ref, flat, rows):
    convert(flat_ref, flat, flat.shape[0], 240)
    from_flat(flat, rows, D, QKVW)
    join_chunks(rows, w_ref)
    for c, w in col_chunks(QKVW):
        wt_ref[c : c + w, :] = nt(eye(w), w_ref[:, c : c + w]).astype(BF)


def forward_kernel(slices, me_ref, *refs):
    x_refs = refs[:slices]
    wt_ref, gain_ref, cos_ref, sin_ref = refs[slices : slices + 4]
    xt_ref, qkv_ref, o_ref, lse_ref, krow = refs[-5:]
    _, _, span = x_refs[0].shape
    length = slices * span
    me = me_ref[0]
    for k in range(slices):
        at = pl.multiple_of((me ^ k) * span, span)
        xt_ref[0, :, pl.ds(at, span)] = x_refs[k][0]
    gain = gain_ref[...]

    @pl.loop(0, length, step=TILE)
    def _(start):
        tok = pl.ds(pl.multiple_of(start, TILE), TILE)
        x = xt_ref[0, :, tok].astype(F32)
        normed = (x * inverse_rms(x) * gain).astype(BF)
        proj = nn(wt_ref[...], normed)
        cos = cos_ref[:, tok]
        sin = sin_ref[:, tok]
        for j in range(HEADS + KV_HEADS):
            u1 = proj[j * HEAD : j * HEAD + HALF]
            u2 = proj[j * HEAD + HALF : (j + 1) * HEAD]
            r1 = (u1 * cos - u2 * sin).astype(BF)
            r2 = (u2 * cos + u1 * sin).astype(BF)
            if j < HEADS:
                r1 = r1 * jnp.asarray(0.125, BF)
                r2 = r2 * jnp.asarray(0.125, BF)
            qkv_ref[0, j * HEAD : j * HEAD + HALF, tok] = r1
            qkv_ref[0, j * HEAD + HALF : (j + 1) * HEAD, tok] = r2
        qkv_ref[0, V0:, tok] = proj[V0:].astype(BF)
        for j in range(KV_HEADS):
            krow[j, tok, :] = unflip(qkv_ref[0, KV0 + j * HEAD : KV0 + (j + 1) * HEAD, tok])

    keep = tri_mask(TILE)

    def head(h, carry):
        kv = h // GROUP
        rows = pl.ds(pl.multiple_of(h * HEAD, HEAD), HEAD)
        vrows = pl.ds(pl.multiple_of(V0 + kv * HEAD, HEAD), HEAD)
        for t in range(0, length, TILE):
            cols = slice(t, t + TILE)
            q = qkv_ref[0, rows, cols]
            last = jnp.where(keep, nn(krow[kv, cols, :], q), NEG_FILL)
            top = jnp.max(last, axis=0, keepdims=True)
            if t:
                before = nn(krow[kv, 0:t, :], q)
                top = jnp.maximum(top, jnp.max(before, axis=0, keepdims=True))
            e = jnp.exp(last - top)
            total = jnp.sum(e, axis=0, keepdims=True)
            acc = nn(qkv_ref[0, vrows, cols], e.astype(BF))
            if t:
                e = jnp.exp(before - top)
                total = total + jnp.sum(e, axis=0, keepdims=True)
                acc = acc + nn(qkv_ref[0, vrows, 0:t], e.astype(BF))
            o_ref[0, rows, cols] = (acc * (1.0 / total)).astype(BF)
            lse_ref[0, kv, pl.ds(h % GROUP, 1), cols] = top + jnp.log(total)
        return carry

    lax.fori_loop(0, HEADS, head, 0)


def middle_kernel(
    me_ref, xt_ref, o_ref, dy_ref, fo_ref, fgu_ref, fd_ref, gain_ref,
    out_ref, dr_ref, do_ref, delta_ref, gout_ref, ggu_ref, gdown_ref, gg_ref,
    wo_ref, wgu_ref, wd_ref, wot, wgut, wdt, aout, agu, adown,
):
    step = pl.program_id(0) * pl.num_programs(1) + pl.program_id(1)
    last = pl.num_programs(0) * pl.num_programs(1) - 1

    @pl.when(step == 0)
    def _():
        convert(fgu_ref, ggu_ref, fgu_ref.shape[0], 256)
        from_flat(ggu_ref, wgu_ref, D, 2 * FF)
        convert(fd_ref, gdown_ref, fd_ref.shape[0], 256)
        from_flat(gdown_ref, adown, FF, D)
        join_chunks(adown, wd_ref)
        convert(fo_ref, gout_ref, fo_ref.shape[0], 96)
        from_flat(gout_ref, aout, D, D)
        join_chunks(aout, wo_ref)

        @pl.loop(0, 2 * FF, step=TILE)
        def _(c):
            at = pl.ds(pl.multiple_of(c, TILE), TILE)
            wgut[at, :] = nt(eye(TILE), wgu_ref[:, at]).astype(BF)

        for c, w in col_chunks(D):
            wdt[c : c + w, :] = nt(eye(w), wd_ref[:, c : c + w]).astype(BF)
            wot[c : c + w, :] = nt(eye(w), wo_ref[:, c : c + w]).astype(BF)
        clear(aout, 64)
        clear(agu, 16)
        clear(adown, 64)
        gg_ref[...] = jnp.zeros_like(gg_ref)

    gain = gain_ref[...]
    o = o_ref[0]
    r = xt_ref[0].astype(F32) + nn(wot[...], o)
    inv = inverse_rms(r)
    n = r * inv
    h = (n * gain).astype(BF)
    a = nn(wgut[0:FF, :], h)
    u = nn(wgut[FF:, :], h)
    sg = 1.0 / (1.0 + jnp.exp(-a))
    act = a * sg
    m = (act * u).astype(BF)
    out_ref[0, 0] = (r + nn(wdt[...], m)).astype(BF)
    dyt = dy_ref[0, 0]
    add_chunks(adown, nt(m, dyt))
    dm = nn(wd_ref[...], dyt)
    da = (dm * u * sg * (1.0 + a * (1.0 - sg))).astype(BF)
    du = (dm * act).astype(BF)
    agu[:, 0:FF] += nt(h, da)
    agu[:, FF:] += nt(h, du)
    dh = nn(wgu_ref[:, 0:FF], da) + nn(wgu_ref[:, FF:], du)
    dhn = dh * n
    part = dhn[:, 0:128]
    for c in range(128, dhn.shape[1], 128):
        part = part + dhn[:, c : c + 128]
    gg_ref[...] += part
    e = dh * gain
    dr = dyt.astype(F32) + inv * (e - n * (jnp.sum(e * n, axis=0, keepdims=True) * (1.0 / D)))
    dr_ref[0] = dr
    db = dr.astype(BF)
    add_chunks(aout, nt(o, db))
    do = nn(wo_ref[...], db).astype(BF)
    do_ref[0] = do
    prod = do.astype(F32) * o.astype(F32)
    for j in range(HEADS):
        delta_ref[0, j // GROUP, j % GROUP : j % GROUP + 1, :] = jnp.sum(prod[j * HEAD : (j + 1) * HEAD], axis=0, keepdims=True)

    @pl.when(step == last)
    def _():
        to_flat(aout, gout_ref, D, D)
        to_flat(agu, ggu_ref, D, 2 * FF)
        to_flat(adown, gdown_ref, FF, D)


def attend_back_kernel(
    me_ref, q_ref, k_ref, v_ref, do_ref, lse_ref, delta_ref, cos_ref, sin_ref, dp_ref, krow, vrow, grads
):
    length = q_ref.shape[2]
    k0 = GROUP * HEAD
    v0 = k0 + HEAD
    clear(grads, 64)

    @pl.loop(0, length, step=TILE)
    def _(start):
        tok = pl.ds(pl.multiple_of(start, TILE), TILE)
        krow[tok, :] = unflip(k_ref[0, :, tok])
        vrow[tok, :] = unflip(v_ref[0, :, tok])

    keep = tri_mask(TILE)

    def head(h, carry):
        rows = pl.ds(pl.multiple_of(h * HEAD, HEAD), HEAD)
        for t in range(0, length, TILE):
            cols = slice(t, t + TILE)
            q = q_ref[0, rows, cols]
            do = do_ref[0, rows, cols]
            lse = lse_ref[0, 0, pl.ds(h, 1), cols]
            delta = delta_ref[0, 0, pl.ds(h, 1), cols]
            p = jnp.where(keep, jnp.exp(nn(krow[cols, :], q) - lse), 0.0)
            ds = (p * (nn(vrow[cols, :], do) - delta)).astype(BF)
            grads[v0:, cols] += nt(do, p.astype(BF))
            grads[k0:v0, cols] += nt(q, ds)
            dq = nn(k_ref[0, :, cols], ds)
            if t:
                p = jnp.exp(nn(krow[0:t, :], q) - lse)
                ds = (p * (nn(vrow[0:t, :], do) - delta)).astype(BF)
                grads[v0:, 0:t] += nt(do, p.astype(BF))
                grads[k0:v0, 0:t] += nt(q, ds)
                dq = dq + nn(k_ref[0, :, 0:t], ds)
            grads[rows, cols] = dq * 0.125
        return carry

    lax.fori_loop(0, GROUP, head, 0)

    @pl.loop(0, length, step=TILE)
    def _(start):
        tok = pl.ds(pl.multiple_of(start, TILE), TILE)
        cos = cos_ref[:, tok]
        sin = sin_ref[:, tok]
        for j in range(GROUP + 1):
            one = slice(j * HEAD, j * HEAD + HALF)
            two = slice(j * HEAD + HALF, (j + 1) * HEAD)
            g1 = grads[one, tok]
            g2 = grads[two, tok]
            dp_ref[0, one, tok] = (g1 * cos + g2 * sin).astype(BF)
            dp_ref[0, two, tok] = (g2 * cos - g1 * sin).astype(BF)
        dp_ref[0, v0:, tok] = grads[v0:, tok].astype(BF)


def project_back_kernel(me_ref, d0_ref, d1_ref, d2_ref, xt_ref, dr_ref, w_ref, gain_ref, *refs):
    gin_ref, gqkv_ref, gg_ref, acc = refs[-4:]

    @pl.when(pl.program_id(0) == 0)
    def _():
        if len(refs) > 4:
            from_flat(refs[0], acc, D, QKVW)
            gg_ref[...] = refs[1][...]
        else:
            clear(acc, 64)
            gg_ref[...] = jnp.zeros_like(gg_ref)

    groups = (d0_ref, d1_ref, d2_ref)
    k0 = GROUP * HEAD
    v0 = k0 + HEAD
    dp = jnp.concatenate(
        [g[0, 0:k0, :] for g in groups] + [g[0, k0:v0, :] for g in groups] + [g[0, v0:, :] for g in groups], axis=0
    )
    x = xt_ref[0].astype(F32)
    inv = inverse_rms(x)
    n = x * inv
    gain = gain_ref[...]
    add_chunks(acc, nt((n * gain).astype(BF), dp))
    dh = nn(w_ref[...], dp)
    dhn = dh * n
    part = dhn[:, 0:128]
    for c in range(128, dhn.shape[1], 128):
        part = part + dhn[:, c : c + 128]
    gg_ref[...] += part
    e = dh * gain
    gin = dr_ref[0] + inv * (e - n * (jnp.sum(e * n, axis=0, keepdims=True) * (1.0 / D)))
    gin_ref[0] = gin.astype(BF)

    @pl.when(pl.program_id(0) == pl.num_programs(0) - 1)
    def _():
        to_flat(acc, gqkv_ref, D, QKVW)


WHOLE = pl.BlockSpec(memory_space=pltpu.VMEM)


def prepare(flat):
    return pl.pallas_call(
        prepare_kernel,
        in_specs=[WHOLE],
        out_specs=[WHOLE, WHOLE],
        out_shape=[jax.ShapeDtypeStruct((D, QKVW), BF), jax.ShapeDtypeStruct((QKVW, D), BF)],
        scratch_shapes=[pltpu.VMEM(flat.shape, F32), pltpu.VMEM((8, D, 128), F32)],
        compiler_params=pltpu.CompilerParams(vmem_limit_bytes=24 << 20),
        cost_estimate=pl.CostEstimate(flops=2 * D * D * QKVW, bytes_accessed=6 * D * QKVW, transcendentals=0),
        name="prepare",
    )(flat)


def attention_forward(seq, me, x_parts, wt, gain, cos, sin, before):
    slices = len(x_parts)
    seqs, _, span = x_parts[0].shape
    length = slices * span
    by_seq = lambda rows: pl.BlockSpec((1, rows, length), lambda s, me: (seq, 0, 0))
    stats = pl.BlockSpec((1, KV_HEADS, GROUP, length), lambda s, me: (seq, 0, 0, 0))
    n_in = 1 + slices + 4
    return pl.pallas_call(
        functools.partial(forward_kernel, slices),
        grid_spec=pltpu.PrefetchScalarGridSpec(
            num_scalar_prefetch=1,
            grid=(1,),
            in_specs=[
                *[pl.BlockSpec((1, D, span), lambda s, me: (seq, 0, 0))] * slices,
                WHOLE, WHOLE, WHOLE, WHOLE,
                *[pl.BlockSpec(memory_space=pl.ANY)] * len(before),
            ],
            out_specs=[by_seq(D), by_seq(QKVW), by_seq(D), stats],
            scratch_shapes=[pltpu.VMEM((KV_HEADS, length, HEAD), BF)],
        ),
        out_shape=[
            jax.ShapeDtypeStruct((seqs, D, length), BF),
            jax.ShapeDtypeStruct((seqs, QKVW, length), BF),
            jax.ShapeDtypeStruct((seqs, D, length), BF),
            jax.ShapeDtypeStruct((seqs, KV_HEADS, GROUP, length), F32),
        ],
        input_output_aliases={n_in + i: i for i in range(len(before))},
        compiler_params=pltpu.CompilerParams(vmem_limit_bytes=40 << 20),
        cost_estimate=pl.CostEstimate(
            flops=2 * length * D * QKVW + 16 * HEADS * length * length * HEAD,
            bytes_accessed=length * 7000,
            transcendentals=HEADS * length * length // 2,
        ),
        name="attention_forward",
    )(me, *x_parts, wt, gain, cos, sin, *before)


def middle(me, xt, o, dy_stack, wo, wgu, wd, gain):
    slices, seqs, _, span = dy_stack.shape
    length = slices * span
    stats = pl.BlockSpec((1, KV_HEADS, GROUP, span), lambda s, k, me: (s, 0, 0, k ^ me[0]))
    tile = lambda rows: pl.BlockSpec((1, rows, span), lambda s, k, me: (s, 0, k ^ me[0]))
    stacked = pl.BlockSpec((1, 1, D, span), lambda s, k, me: (k, s, 0, 0))
    return pl.pallas_call(
        middle_kernel,
        grid_spec=pltpu.PrefetchScalarGridSpec(
            num_scalar_prefetch=1,
            grid=(seqs, slices),
            in_specs=[tile(D), tile(D), stacked, WHOLE, WHOLE, WHOLE, WHOLE],
            out_specs=[stacked, tile(D), tile(D), stats, WHOLE, WHOLE, WHOLE, WHOLE],
            scratch_shapes=[
                pltpu.VMEM((D, D), BF),
                pltpu.VMEM((D, 2 * FF), BF),
                pltpu.VMEM((FF, D), BF),
                pltpu.VMEM((D, D), BF),
                pltpu.VMEM((2 * FF, D), BF),
                pltpu.VMEM((D, FF), BF),
                pltpu.VMEM((5, D, 128), F32),
                pltpu.VMEM((D, 2 * FF), F32),
                pltpu.VMEM((5, FF, 128), F32),
            ],
        ),
        out_shape=[
            jax.ShapeDtypeStruct((slices, seqs, D, span), BF),
            jax.ShapeDtypeStruct((seqs, D, length), F32),
            jax.ShapeDtypeStruct((seqs, D, length), BF),
            jax.ShapeDtypeStruct((seqs, KV_HEADS, GROUP, length), F32),
            jax.ShapeDtypeStruct((D * D // 128, 128), F32),
            jax.ShapeDtypeStruct((D * 2 * FF // 128, 128), F32),
            jax.ShapeDtypeStruct((FF * D // 128, 128), F32),
            jax.ShapeDtypeStruct((D, 128), F32),
        ],
        compiler_params=pltpu.CompilerParams(vmem_limit_bytes=60 << 20),
        cost_estimate=pl.CostEstimate(
            flops=seqs * length * 6 * (D * D + 3 * D * FF),
            bytes_accessed=seqs * length * 8000 + 12000000,
            transcendentals=seqs * length * FF,
        ),
        name="middle",
    )(me, xt, o, dy_stack, wo, wgu, wd, gain)


def attend_back(first, count, me, qkv, do, lse, delta, cos, sin):
    length = qkv.shape[2]
    width = (GROUP + 2) * HEAD
    at = lambda p: ((first + p) // KV_HEADS, (first + p) % KV_HEADS)
    rows = lambda n, base: pl.BlockSpec((1, n, length), lambda p, me: (at(p)[0], base + at(p)[1], 0))
    stats = pl.BlockSpec((1, 1, GROUP, length), lambda p, me: (*at(p), 0, 0))
    return pl.pallas_call(
        attend_back_kernel,
        grid_spec=pltpu.PrefetchScalarGridSpec(
            num_scalar_prefetch=1,
            grid=(count,),
            in_specs=[
                rows(GROUP * HEAD, 0), rows(HEAD, KV0 // HEAD), rows(HEAD, V0 // HEAD), rows(GROUP * HEAD, 0),
                stats, stats, WHOLE, WHOLE,
            ],
            out_specs=pl.BlockSpec((1, width, length), lambda p, me: (p, 0, 0)),
            scratch_shapes=[
                pltpu.VMEM((length, HEAD), BF),
                pltpu.VMEM((length, HEAD), BF),
                pltpu.VMEM((width, length), F32),
            ],
        ),
        out_shape=jax.ShapeDtypeStruct((count, width, length), BF),
        compiler_params=pltpu.CompilerParams(vmem_limit_bytes=40 << 20),
        cost_estimate=pl.CostEstimate(
            flops=count * 30 * GROUP * length * length * HEAD,
            bytes_accessed=count * length * 3000,
            transcendentals=count * GROUP * length * length // 2,
        ),
        name="attend_back",
    )(me, qkv, qkv, qkv, do, lse, delta, cos, sin)


def project_back(seq, me, pairs, xt, dr, w, gain, slices, earlier):
    length = xt.shape[2]
    span = length // slices
    width = (GROUP + 2) * HEAD
    tile = pl.BlockSpec((1, D, span), lambda k, me: (seq, 0, k ^ me[0]))
    return pl.pallas_call(
        project_back_kernel,
        grid_spec=pltpu.PrefetchScalarGridSpec(
            num_scalar_prefetch=1,
            grid=(slices,),
            in_specs=[
                *[pl.BlockSpec((1, width, span), lambda k, me, i=i: (i, 0, k ^ me[0])) for _, i in pairs],
                tile, tile, WHOLE, WHOLE, *[WHOLE] * len(earlier),
            ],
            out_specs=[pl.BlockSpec((1, D, span), lambda k, me: (k, 0, 0)), WHOLE, WHOLE],
            scratch_shapes=[pltpu.VMEM((8, D, 128), F32)],
        ),
        out_shape=[
            jax.ShapeDtypeStruct((slices, D, span), BF),
            jax.ShapeDtypeStruct((D * QKVW // 128, 128), F32),
            jax.ShapeDtypeStruct((D, 128), F32),
        ],
        compiler_params=pltpu.CompilerParams(vmem_limit_bytes=32 << 20),
        cost_estimate=pl.CostEstimate(
            flops=8 * length * D * QKVW, bytes_accessed=length * 8000 + 4000000, transcendentals=0
        ),
        name="project_back",
    )(me, *[array for array, _ in pairs], xt, dr, w, gain, *earlier)


def partner(array, name, bits):
    return lax.ppermute(array, name, [(i, i ^ bits) for i in range(lax.axis_size(name))])


def digit_of(name, stride, count):
    return (lax.axis_index(name) // stride) % count


def in_order(parts, digit):
    bit = 1
    while bit < len(parts):
        swap = (digit & bit) != 0
        parts = [jnp.where(swap, parts[k ^ bit], parts[k]) for k in range(len(parts))]
        bit *= 2
    return parts


def after(value, *others):
    others = [other for other in others if other is not None]
    return lax.optimization_barrier((value, *others))[0] if others else value


def gather_digit(array, name, stride, count, hold=None):
    shape = array.shape
    step = 1
    while step < count:
        parts = [array, after(partner(array, name, step * stride), hold if 2 * step >= count else None)]
        array = jnp.stack(in_order(parts, digit_of(name, step * stride, 2)))
        step *= 2
    return array.reshape(count, *shape)


def sum_digit(terms, axis, name, stride, count, dtype, hold=None):
    digit = digit_of(name, stride, count)
    total = lax.dynamic_index_in_dim(terms, digit, axis, keepdims=False).astype(F32)
    for k in range(1, count):
        piece = lax.dynamic_index_in_dim(terms, digit ^ k, axis, keepdims=False).astype(BF)
        total = total + after(partner(piece, name, k * stride), hold).astype(F32)
    return total.astype(dtype)


def local(tokens, w_qkv, w_out, w_gate_up, w_down, gains, cotangent):
    slices = lax.axis_size("ctx")
    across = lax.axis_size("dp")
    world = slices * across
    span = tokens.shape[1]
    seqs = tokens.shape[0] // slices
    length = slices * span
    ctx = lax.axis_index("ctx")
    me = ctx.astype(jnp.int32).reshape(1)
    nz = min(4, across)
    nx = across // nz
    ny = slices // 2
    core = ("ctx", 1, 2)
    y = ("ctx", 2, ny)
    x = ("dp", 1, nx)
    z = ("dp", nx, nz)

    def blocks(array):
        grouped = array.transpose(0, 2, 1).reshape(slices, seqs, D, span)
        return [lax.dynamic_index_in_dim(grouped, ctx ^ k, 0, keepdims=False) for k in range(slices)]

    def receive(parts, hold, which):
        for k in which:
            parts[k] = after(partner(parts[k], "ctx", k), hold)
        return [parts[k] for k in which]

    everyone = range(1, slices)
    near = [k for k in everyone if k < 3]
    far = [k for k in everyone if k >= 3]

    def placed(stack):
        return stack.reshape(tokens.shape[0], D, span).transpose(0, 2, 1)

    def as_rows(shard):
        return jnp.pad(shard, (0, -shard.shape[0] % 1024)).reshape(-1, 128)

    def whole_flat(stack, order, size):
        stack = stack.transpose(*[order.index(d) for d in "zxyc"], 4, 5)
        return stack.reshape(world, -1, 128)[:, : -(-size // 128)].reshape(world, -1)[:, :size].reshape(-1, 128)

    def shares(flat):
        if flat.size % (world * 128) == 0:
            return flat.reshape(nz, nx, ny, 2, -1, 128)
        rows = flat.reshape(world, -1)
        return jnp.pad(rows, ((0, 0), (0, -rows.shape[1] % 128))).reshape(nz, nx, ny, 2, -1, 128)

    n_qkv = w_qkv.shape[0]
    n_gain = gains.shape[0]
    early = as_rows(jnp.concatenate([w_qkv, gains]))
    for digit in (y, x, z, core):
        early = gather_digit(early, *digit)
    early = early.transpose(1, 2, 3, 0, 4, 5).reshape(world, -1, 128)
    flat_qkv = early[:, : n_qkv // 128].reshape(-1, 128) if n_qkv % 128 == 0 else early.reshape(world, -1)[:, :n_qkv].reshape(-1, 128)
    gain_all = early.reshape(world, -1)[:, n_qkv : n_qkv + n_gain].reshape(2, D, 1).astype(F32)
    x_parts = blocks(tokens)
    receive(x_parts, None, everyone)
    gu_rows, down_rows = as_rows(w_gate_up), as_rows(w_down)
    rest1 = gather_digit(jnp.concatenate([gu_rows, down_rows, as_rows(w_out)]), *z, flat_qkv)
    gu1 = rest1[:, : gu_rows.shape[0]]
    both1 = rest1[:, gu_rows.shape[0] :]
    cos, sin = rotary_tables(length)
    mat_qkv, mat_qkv_t = prepare(flat_qkv)
    forward = ()
    dy_parts = blocks(after(cotangent, gu1, both1))
    for s in range(seqs):
        order = after(me, gu1, both1) if s == 0 else after(me, gu2, both2, *dy_near)
        forward = attention_forward(s, order, x_parts, mat_qkv_t, gain_all[0], cos, sin, forward)
        if s == 0:
            gu2 = gather_digit(gu1, *y, forward[3])
            both2 = gather_digit(both1, *x, forward[3])
            dy_near = receive(dy_parts, forward[3], near)
    xt, qkv, o, lse = forward
    gu3 = gather_digit(gu2, *x, lse)
    both3 = gather_digit(both2, *y, lse)
    flat_gu = whole_flat(gather_digit(gu3, *core, lse), "cxyz", w_gate_up.shape[0])
    both4 = gather_digit(both3, *core, lse)
    flat_down = whole_flat(both4[..., : down_rows.shape[0], :], "cyxz", w_down.shape[0])
    flat_out = whole_flat(both4[..., down_rows.shape[0] :, :], "cyxz", w_out.shape[0])
    receive(dy_parts, lse, far)
    dy_stack = jnp.stack(dy_parts)
    out_stack, dr, do, delta, g_out, g_gu, g_down, gg2 = middle(
        me, xt, o, dy_stack, flat_out, flat_gu, flat_down, gain_all[1]
    )

    n_pairs = seqs * KV_HEADS
    pairs = []
    back = []
    sums = [shares(g) for g in (g_gu, g_down, g_out)]
    gu_count, down_count = sums[0].shape[4], sums[1].shape[4]
    stages = [
        ((3, *core),) * 3,
        ((1, *x), (2, *y)),
        ((1, *y), (1, *x)),
    ]
    order = me
    out_parts = [out_stack[k] for k in range(slices)]
    out_waits = [near, far]

    def advance(hold):
        nonlocal sums
        if stages:
            sums = [sum_digit(r, *how, BF, hold) for r, how in zip(sums, stages.pop(0))]
            sums = [sums[0], jnp.concatenate(sums[1:], axis=-2)]
        return after(me, hold, *sums)

    for first in range(0, n_pairs, 2):
        count = min(2, n_pairs - first)
        dp = attend_back(first, count, order, qkv, do, lse, delta, cos, sin)
        pairs += [(dp, i) for i in range(count)]
        waited = receive(out_parts, dp, out_waits.pop(0)) if out_waits else []
        if first == 0 or n_pairs - first <= 2 or len(pairs) < KV_HEADS * (len(back) + 1):
            order = advance(dp)
        while len(pairs) >= KV_HEADS * (len(back) + 1):
            s = len(back)
            back.append(
                project_back(
                    s, order, pairs[KV_HEADS * s : KV_HEADS * (s + 1)], xt, dr, mat_qkv, gain_all[0], slices,
                    back[-1][1:] if back else (),
                )
            )
            if len(back) < seqs:
                order = advance(back[-1][2])
        order = after(order, *waited)
    while stages:
        advance(None)
    g_qkv, gg1 = back[-1][1:]
    returned = [[b[0][k] for k in range(slices)] for b in back]
    for parts in returned[:-1]:
        g_qkv = after(g_qkv, *receive(parts, gg1, everyone))
    gg = jnp.concatenate([jnp.sum(gg1, axis=1), jnp.sum(gg2, axis=1)])
    late = jnp.concatenate([g_qkv.reshape(world, -1), gg.reshape(world, -1)], axis=1)
    late = sum_digit(shares(late), 3, *core, BF)
    late = sum_digit(late, 1, *x, BF)
    late = sum_digit(late, 1, *y, BF)
    own_late = sum_digit(late, 0, *z, F32).reshape(-1)
    receive(returned[-1], late, everyone)
    own = jnp.concatenate(sums, axis=-2)
    step = nz // 2
    while step:
        own = own.reshape(2, step, *own.shape[1:])
        own = sum_digit(own, 0, "dp", nx * step, 2, BF if step > 1 else F32, late)
        step //= 2
    own = own.reshape(own.shape[-2:])
    out_parts[0] = after(out_parts[0], late)
    output = placed(jnp.stack(in_order(out_parts, ctx)))
    grad_input = placed(jnp.stack([jnp.stack(in_order(parts, ctx)) for parts in returned], axis=1))
    return (
        output,
        grad_input,
        own_late[:n_qkv],
        own[gu_count + down_count :].reshape(-1)[: w_out.shape[0]],
        own[:gu_count].reshape(-1)[: w_gate_up.shape[0]],
        own[gu_count : gu_count + down_count].reshape(-1)[: w_down.shape[0]],
        own_late[n_qkv : n_qkv + n_gain],
    )


def solution(mesh):
    flat = P(("dp", "ctx"))
    rows = P("dp", "ctx", None)
    return jax.shard_map(
        local,
        mesh=mesh,
        in_specs=(rows, flat, flat, flat, flat, flat, rows),
        out_specs=(rows, rows, flat, flat, flat, flat, flat),
        check_vma=False,
    )
```

```python
import functools
import math

import jax
import jax.numpy as jnp
from jax import lax
from jax.experimental import pallas as pl
from jax.experimental.pallas import tpu as pltpu
from jax.sharding import PartitionSpec as P

D = 576
HEADS = 9
KV_HEADS = 3
HEAD = 64
GROUP = HEADS // KV_HEADS
FF = 1536
QKVW = 960
KV0 = D
V0 = D + KV_HEADS * HEAD
HALF = HEAD // 2
TILE = 256

EPSILON = 1e-05
THETA_BASE = 100000.0
NEG_FILL = -1e30
BF = jnp.bfloat16
F32 = jnp.float32


def nn(a, b):
    return lax.dot_general(a, b, (((1,), (0,)), ((), ())), preferred_element_type=F32)


def nt(a, b):
    return lax.dot_general(a, b, (((1,), (1,)), ((), ())), preferred_element_type=F32)


def eye(size):
    r = lax.broadcasted_iota(jnp.int32, (size, size), 0)
    c = lax.broadcasted_iota(jnp.int32, (size, size), 1)
    return jnp.where(r == c, 1.0, 0.0).astype(BF)


def col_chunks(width, step=128):
    return [(c, min(step, width - c)) for c in range(0, width, step)]


def unflip(cols):
    return nt(eye(cols.shape[1]), cols).astype(BF)


def inverse_rms(cols):
    return lax.rsqrt(jnp.sum(cols * cols, axis=0, keepdims=True) * (1.0 / D) + EPSILON)


def rotary_tables(length):
    halves = jnp.arange(0, HEAD, 2).astype(F32) / HEAD
    inverse = jnp.exp(-math.log(THETA_BASE) * halves)
    angles = inverse[:, None] * jnp.arange(length).astype(F32)[None, :]
    return jnp.cos(angles), jnp.sin(angles)


def tri_mask(size):
    key = lax.broadcasted_iota(jnp.int32, (size, size), 0)
    query = lax.broadcasted_iota(jnp.int32, (size, size), 1)
    return key <= query


def lane_low(size):
    return lax.broadcasted_iota(jnp.int32, (size, 128), 1) < 64


def to_flat(rows_ref, flat_ref, rows, width):
    if width % 128 == 0:
        n = width // 128

        @pl.loop(0, n)
        def _(c):
            flat_ref[pl.ds(c, rows, stride=n), :] = rows_ref[:, pl.ds(pl.multiple_of(c * 128, 128), 128)]

        return
    n = 2 * width // 128
    half = rows // 2
    low = lane_low(half)
    even = lambda c: rows_ref[c, pl.ds(0, half, stride=2), :]
    odd = lambda c: pltpu.roll(rows_ref[c, pl.ds(1, half, stride=2), :], 64, 1)
    for c in range(n // 2):
        flat_ref[pl.ds(c, half, stride=n), :] = even(c)
    before = odd(0)
    flat_ref[pl.ds(n // 2, half, stride=n), :] = jnp.where(low, even(n // 2), before)
    for c in range(n // 2):
        after = odd(c + 1)
        flat_ref[pl.ds(n // 2 + 1 + c, half, stride=n), :] = jnp.where(low, before, after)
        before = after


def from_flat(flat_ref, rows_ref, rows, width):
    if width % 128 == 0:
        n = width // 128

        @pl.loop(0, n)
        def _(c):
            rows_ref[:, pl.ds(pl.multiple_of(c * 128, 128), 128)] = flat_ref[
                pl.ds(c, rows, stride=n), :
            ].astype(rows_ref.dtype)

        return
    n = 2 * width // 128
    half = rows // 2
    low = lane_low(half)
    take = lambda c: flat_ref[pl.ds(c, half, stride=n), :]
    for c in range(n // 2 + 1):
        rows_ref[c, pl.ds(0, half, stride=2), :] = take(c)
    before = pltpu.roll(take(n // 2), 64, 1)
    for c in range(n // 2):
        after = pltpu.roll(take(n // 2 + 1 + c), 64, 1)
        rows_ref[c, pl.ds(1, half, stride=2), :] = jnp.where(low, before, after)
        before = after
    rows_ref[n // 2, pl.ds(1, half, stride=2), :] = before


def convert(src_ref, dst_ref, rows, step):
    @pl.loop(0, rows, step=step)
    def _(i):
        at = pl.ds(pl.multiple_of(i, step), step)
        dst_ref[at, :] = src_ref[at, 0 : dst_ref.shape[1]].astype(dst_ref.dtype)


def clear(ref, step):
    @pl.loop(0, ref.shape[-2], step=step)
    def _(i):
        at = pl.ds(pl.multiple_of(i, step), step)
        if len(ref.shape) == 3:
            ref[:, at, :] = jnp.zeros((ref.shape[0], step, ref.shape[2]), ref.dtype)
        else:
            ref[at, :] = jnp.zeros((step, ref.shape[1]), ref.dtype)


def add_chunks(ref, value):
    for c, w in col_chunks(value.shape[1]):
        ref[c // 128, :, 0:w] += value[:, c : c + w]


def join_chunks(src_ref, dst_ref):
    for c, w in col_chunks(dst_ref.shape[1]):
        dst_ref[:, c : c + w] = src_ref[c // 128, :, 0:w].astype(dst_ref.dtype)


def prepare_kernel(flat_ref, w_ref, wt_ref, flat, rows):
    convert(flat_ref, flat, flat.shape[0], 240)
    from_flat(flat, rows, D, QKVW)
    join_chunks(rows, w_ref)
    for c, w in col_chunks(QKVW):
        wt_ref[c : c + w, :] = nt(eye(w), w_ref[:, c : c + w]).astype(BF)


def forward_kernel(slices, me_ref, *refs):
    x_refs = refs[:slices]
    wt_ref, gain_ref, cos_ref, sin_ref = refs[slices : slices + 4]
    xt_ref, qkv_ref, o_ref, lse_ref, krow = refs[-5:]
    _, _, span = x_refs[0].shape
    length = slices * span
    me = me_ref[0]
    for k in range(slices):
        at = pl.multiple_of((me ^ k) * span, span)
        xt_ref[0, :, pl.ds(at, span)] = x_refs[k][0]
    gain = gain_ref[...]

    @pl.loop(0, length, step=TILE)
    def _(start):
        tok = pl.ds(pl.multiple_of(start, TILE), TILE)
        x = xt_ref[0, :, tok].astype(F32)
        normed = (x * inverse_rms(x) * gain).astype(BF)
        proj = nn(wt_ref[...], normed)
        cos = cos_ref[:, tok]
        sin = sin_ref[:, tok]
        for j in range(HEADS + KV_HEADS):
            u1 = proj[j * HEAD : j * HEAD + HALF]
            u2 = proj[j * HEAD + HALF : (j + 1) * HEAD]
            r1 = (u1 * cos - u2 * sin).astype(BF)
            r2 = (u2 * cos + u1 * sin).astype(BF)
            if j < HEADS:
                r1 = r1 * jnp.asarray(0.125, BF)
                r2 = r2 * jnp.asarray(0.125, BF)
            qkv_ref[0, j * HEAD : j * HEAD + HALF, tok] = r1
            qkv_ref[0, j * HEAD + HALF : (j + 1) * HEAD, tok] = r2
        qkv_ref[0, V0:, tok] = proj[V0:].astype(BF)
        for j in range(KV_HEADS):
            krow[j, tok, :] = unflip(qkv_ref[0, KV0 + j * HEAD : KV0 + (j + 1) * HEAD, tok])

    keep = tri_mask(TILE)

    def head(h, carry):
        kv = h // GROUP
        rows = pl.ds(pl.multiple_of(h * HEAD, HEAD), HEAD)
        vrows = pl.ds(pl.multiple_of(V0 + kv * HEAD, HEAD), HEAD)
        for t in range(0, length, TILE):
            cols = slice(t, t + TILE)
            q = qkv_ref[0, rows, cols]
            last = jnp.where(keep, nn(krow[kv, cols, :], q), NEG_FILL)
            top = jnp.max(last, axis=0, keepdims=True)
            if t:
                before = nn(krow[kv, 0:t, :], q)
                top = jnp.maximum(top, jnp.max(before, axis=0, keepdims=True))
            e = jnp.exp(last - top)
            total = jnp.sum(e, axis=0, keepdims=True)
            acc = nn(qkv_ref[0, vrows, cols], e.astype(BF))
            if t:
                e = jnp.exp(before - top)
                total = total + jnp.sum(e, axis=0, keepdims=True)
                acc = acc + nn(qkv_ref[0, vrows, 0:t], e.astype(BF))
            o_ref[0, rows, cols] = (acc * (1.0 / total)).astype(BF)
            lse_ref[0, kv, pl.ds(h % GROUP, 1), cols] = top + jnp.log(total)
        return carry

    lax.fori_loop(0, HEADS, head, 0)


def middle_kernel(
    me_ref, xt_ref, o_ref, dy_ref, fo_ref, fgu_ref, fd_ref, gain_ref,
    out_ref, dr_ref, do_ref, delta_ref, gout_ref, ggu_ref, gdown_ref, gg_ref,
    wo_ref, wgu_ref, wd_ref, wot, wgut, wdt, aout, agu, adown,
):
    step = pl.program_id(0) * pl.num_programs(1) + pl.program_id(1)
    last = pl.num_programs(0) * pl.num_programs(1) - 1

    @pl.when(step == 0)
    def _():
        convert(fgu_ref, ggu_ref, fgu_ref.shape[0], 256)
        from_flat(ggu_ref, wgu_ref, D, 2 * FF)
        convert(fd_ref, gdown_ref, fd_ref.shape[0], 256)
        from_flat(gdown_ref, adown, FF, D)
        join_chunks(adown, wd_ref)
        convert(fo_ref, gout_ref, fo_ref.shape[0], 96)
        from_flat(gout_ref, aout, D, D)
        join_chunks(aout, wo_ref)

        @pl.loop(0, 2 * FF, step=TILE)
        def _(c):
            at = pl.ds(pl.multiple_of(c, TILE), TILE)
            wgut[at, :] = nt(eye(TILE), wgu_ref[:, at]).astype(BF)

        for c, w in col_chunks(D):
            wdt[c : c + w, :] = nt(eye(w), wd_ref[:, c : c + w]).astype(BF)
            wot[c : c + w, :] = nt(eye(w), wo_ref[:, c : c + w]).astype(BF)
        clear(aout, 64)
        clear(agu, 16)
        clear(adown, 64)
        gg_ref[...] = jnp.zeros_like(gg_ref)

    gain = gain_ref[...]
    o = o_ref[0]
    r = xt_ref[0].astype(F32) + nn(wot[...], o)
    inv = inverse_rms(r)
    n = r * inv
    h = (n * gain).astype(BF)
    a = nn(wgut[0:FF, :], h)
    u = nn(wgut[FF:, :], h)
    sg = 1.0 / (1.0 + jnp.exp(-a))
    act = a * sg
    m = (act * u).astype(BF)
    out_ref[0, 0] = (r + nn(wdt[...], m)).astype(BF)
    dyt = dy_ref[0, 0]
    add_chunks(adown, nt(m, dyt))
    dm = nn(wd_ref[...], dyt)
    da = (dm * u * sg * (1.0 + a * (1.0 - sg))).astype(BF)
    du = (dm * act).astype(BF)
    agu[:, 0:FF] += nt(h, da)
    agu[:, FF:] += nt(h, du)
    dh = nn(wgu_ref[:, 0:FF], da) + nn(wgu_ref[:, FF:], du)
    dhn = dh * n
    part = dhn[:, 0:128]
    for c in range(128, dhn.shape[1], 128):
        part = part + dhn[:, c : c + 128]
    gg_ref[...] += part
    e = dh * gain
    dr = dyt.astype(F32) + inv * (e - n * (jnp.sum(e * n, axis=0, keepdims=True) * (1.0 / D)))
    dr_ref[0] = dr.astype(BF)
    db = dr.astype(BF)
    add_chunks(aout, nt(o, db))
    do = nn(wo_ref[...], db).astype(BF)
    do_ref[0] = do
    prod = do.astype(F32) * o.astype(F32)
    for j in range(HEADS):
        delta_ref[0, j // GROUP, j % GROUP : j % GROUP + 1, :] = jnp.sum(prod[j * HEAD : (j + 1) * HEAD], axis=0, keepdims=True)

    @pl.when(step == last)
    def _():
        to_flat(aout, gout_ref, D, D)
        to_flat(agu, ggu_ref, D, 2 * FF)
        to_flat(adown, gdown_ref, FF, D)


def attend_back_kernel(
    me_ref, q_ref, k_ref, v_ref, do_ref, lse_ref, delta_ref, cos_ref, sin_ref, dp_ref, krow, vrow, grads
):
    length = q_ref.shape[2]
    k0 = GROUP * HEAD
    v0 = k0 + HEAD
    clear(grads, 64)

    @pl.loop(0, length, step=TILE)
    def _(start):
        tok = pl.ds(pl.multiple_of(start, TILE), TILE)
        krow[tok, :] = unflip(k_ref[0, :, tok])
        vrow[tok, :] = unflip(v_ref[0, :, tok])

    keep = tri_mask(TILE)

    def head(h, carry):
        rows = pl.ds(pl.multiple_of(h * HEAD, HEAD), HEAD)
        for t in range(0, length, TILE):
            cols = slice(t, t + TILE)
            q = q_ref[0, rows, cols]
            do = do_ref[0, rows, cols]
            lse = lse_ref[0, 0, pl.ds(h, 1), cols]
            delta = delta_ref[0, 0, pl.ds(h, 1), cols]
            p = jnp.where(keep, jnp.exp(nn(krow[cols, :], q) - lse), 0.0)
            ds = (p * (nn(vrow[cols, :], do) - delta)).astype(BF)
            grads[v0:, cols] += nt(do, p.astype(BF))
            grads[k0:v0, cols] += nt(q, ds)
            dq = nn(k_ref[0, :, cols], ds)
            if t:
                p = jnp.exp(nn(krow[0:t, :], q) - lse)
                ds = (p * (nn(vrow[0:t, :], do) - delta)).astype(BF)
                grads[v0:, 0:t] += nt(do, p.astype(BF))
                grads[k0:v0, 0:t] += nt(q, ds)
                dq = dq + nn(k_ref[0, :, 0:t], ds)
            grads[rows, cols] = dq * 0.125
        return carry

    lax.fori_loop(0, GROUP, head, 0)

    @pl.loop(0, length, step=TILE)
    def _(start):
        tok = pl.ds(pl.multiple_of(start, TILE), TILE)
        cos = cos_ref[:, tok]
        sin = sin_ref[:, tok]
        for j in range(GROUP + 1):
            one = slice(j * HEAD, j * HEAD + HALF)
            two = slice(j * HEAD + HALF, (j + 1) * HEAD)
            g1 = grads[one, tok]
            g2 = grads[two, tok]
            dp_ref[0, one, tok] = (g1 * cos + g2 * sin).astype(BF)
            dp_ref[0, two, tok] = (g2 * cos - g1 * sin).astype(BF)
        dp_ref[0, v0:, tok] = grads[v0:, tok].astype(BF)


def project_back_kernel(me_ref, d0_ref, d1_ref, d2_ref, xt_ref, dr_ref, w_ref, gain_ref, *refs):
    gin_ref, gqkv_ref, gg_ref, acc = refs[-4:]

    @pl.when(pl.program_id(0) == 0)
    def _():
        if len(refs) > 4:
            from_flat(refs[0], acc, D, QKVW)
            gg_ref[...] = refs[1][...]
        else:
            clear(acc, 64)
            gg_ref[...] = jnp.zeros_like(gg_ref)

    groups = (d0_ref, d1_ref, d2_ref)
    k0 = GROUP * HEAD
    v0 = k0 + HEAD
    dp = jnp.concatenate(
        [g[0, 0:k0, :] for g in groups] + [g[0, k0:v0, :] for g in groups] + [g[0, v0:, :] for g in groups], axis=0
    )
    x = xt_ref[0].astype(F32)
    inv = inverse_rms(x)
    n = x * inv
    gain = gain_ref[...]
    add_chunks(acc, nt((n * gain).astype(BF), dp))
    dh = nn(w_ref[...], dp)
    dhn = dh * n
    part = dhn[:, 0:128]
    for c in range(128, dhn.shape[1], 128):
        part = part + dhn[:, c : c + 128]
    gg_ref[...] += part
    e = dh * gain
    gin = dr_ref[0].astype(F32) + inv * (e - n * (jnp.sum(e * n, axis=0, keepdims=True) * (1.0 / D)))
    gin_ref[0] = gin.astype(BF)

    @pl.when(pl.program_id(0) == pl.num_programs(0) - 1)
    def _():
        to_flat(acc, gqkv_ref, D, QKVW)


WHOLE = pl.BlockSpec(memory_space=pltpu.VMEM)


def prepare(flat):
    return pl.pallas_call(
        prepare_kernel,
        in_specs=[WHOLE],
        out_specs=[WHOLE, WHOLE],
        out_shape=[jax.ShapeDtypeStruct((D, QKVW), BF), jax.ShapeDtypeStruct((QKVW, D), BF)],
        scratch_shapes=[pltpu.VMEM(flat.shape, F32), pltpu.VMEM((8, D, 128), F32)],
        compiler_params=pltpu.CompilerParams(vmem_limit_bytes=24 << 20),
        cost_estimate=pl.CostEstimate(flops=2 * D * D * QKVW, bytes_accessed=6 * D * QKVW, transcendentals=0),
        name="prepare",
    )(flat)


def attention_forward(seq, me, x_parts, wt, gain, cos, sin, before):
    slices = len(x_parts)
    seqs, _, span = x_parts[0].shape
    length = slices * span
    by_seq = lambda rows: pl.BlockSpec((1, rows, length), lambda s, me: (seq, 0, 0))
    stats = pl.BlockSpec((1, KV_HEADS, GROUP, length), lambda s, me: (seq, 0, 0, 0))
    n_in = 1 + slices + 4
    return pl.pallas_call(
        functools.partial(forward_kernel, slices),
        grid_spec=pltpu.PrefetchScalarGridSpec(
            num_scalar_prefetch=1,
            grid=(1,),
            in_specs=[
                *[pl.BlockSpec((1, D, span), lambda s, me: (seq, 0, 0))] * slices,
                WHOLE, WHOLE, WHOLE, WHOLE,
                *[pl.BlockSpec(memory_space=pl.ANY)] * len(before),
            ],
            out_specs=[by_seq(D), by_seq(QKVW), by_seq(D), stats],
            scratch_shapes=[pltpu.VMEM((KV_HEADS, length, HEAD), BF)],
        ),
        out_shape=[
            jax.ShapeDtypeStruct((seqs, D, length), BF),
            jax.ShapeDtypeStruct((seqs, QKVW, length), BF),
            jax.ShapeDtypeStruct((seqs, D, length), BF),
            jax.ShapeDtypeStruct((seqs, KV_HEADS, GROUP, length), F32),
        ],
        input_output_aliases={n_in + i: i for i in range(len(before))},
        compiler_params=pltpu.CompilerParams(vmem_limit_bytes=40 << 20),
        cost_estimate=pl.CostEstimate(
            flops=2 * length * D * QKVW + 16 * HEADS * length * length * HEAD,
            bytes_accessed=length * 7000,
            transcendentals=HEADS * length * length // 2,
        ),
        name="attention_forward",
    )(me, *x_parts, wt, gain, cos, sin, *before)


def middle(me, xt, o, dy_stack, wo, wgu, wd, gain):
    slices, seqs, _, span = dy_stack.shape
    length = slices * span
    stats = pl.BlockSpec((1, KV_HEADS, GROUP, span), lambda s, k, me: (s, 0, 0, k ^ me[0]))
    tile = lambda rows: pl.BlockSpec((1, rows, span), lambda s, k, me: (s, 0, k ^ me[0]))
    stacked = pl.BlockSpec((1, 1, D, span), lambda s, k, me: (k, s, 0, 0))
    return pl.pallas_call(
        middle_kernel,
        grid_spec=pltpu.PrefetchScalarGridSpec(
            num_scalar_prefetch=1,
            grid=(seqs, slices),
            in_specs=[tile(D), tile(D), stacked, WHOLE, WHOLE, WHOLE, WHOLE],
            out_specs=[stacked, tile(D), tile(D), stats, WHOLE, WHOLE, WHOLE, WHOLE],
            scratch_shapes=[
                pltpu.VMEM((D, D), BF),
                pltpu.VMEM((D, 2 * FF), BF),
                pltpu.VMEM((FF, D), BF),
                pltpu.VMEM((D, D), BF),
                pltpu.VMEM((2 * FF, D), BF),
                pltpu.VMEM((D, FF), BF),
                pltpu.VMEM((5, D, 128), F32),
                pltpu.VMEM((D, 2 * FF), F32),
                pltpu.VMEM((5, FF, 128), F32),
            ],
        ),
        out_shape=[
            jax.ShapeDtypeStruct((slices, seqs, D, span), BF),
            jax.ShapeDtypeStruct((seqs, D, length), BF),
            jax.ShapeDtypeStruct((seqs, D, length), BF),
            jax.ShapeDtypeStruct((seqs, KV_HEADS, GROUP, length), F32),
            jax.ShapeDtypeStruct((D * D // 128, 128), F32),
            jax.ShapeDtypeStruct((D * 2 * FF // 128, 128), F32),
            jax.ShapeDtypeStruct((FF * D // 128, 128), F32),
            jax.ShapeDtypeStruct((D, 128), F32),
        ],
        compiler_params=pltpu.CompilerParams(vmem_limit_bytes=60 << 20),
        cost_estimate=pl.CostEstimate(
            flops=seqs * length * 6 * (D * D + 3 * D * FF),
            bytes_accessed=seqs * length * 8000 + 12000000,
            transcendentals=seqs * length * FF,
        ),
        name="middle",
    )(me, xt, o, dy_stack, wo, wgu, wd, gain)


def attend_back(first, count, me, qkv, do, lse, delta, cos, sin):
    length = qkv.shape[2]
    width = (GROUP + 2) * HEAD
    at = lambda p: ((first + p) // KV_HEADS, (first + p) % KV_HEADS)
    rows = lambda n, base: pl.BlockSpec((1, n, length), lambda p, me: (at(p)[0], base + at(p)[1], 0))
    stats = pl.BlockSpec((1, 1, GROUP, length), lambda p, me: (*at(p), 0, 0))
    return pl.pallas_call(
        attend_back_kernel,
        grid_spec=pltpu.PrefetchScalarGridSpec(
            num_scalar_prefetch=1,
            grid=(count,),
            in_specs=[
                rows(GROUP * HEAD, 0), rows(HEAD, KV0 // HEAD), rows(HEAD, V0 // HEAD), rows(GROUP * HEAD, 0),
                stats, stats, WHOLE, WHOLE,
            ],
            out_specs=pl.BlockSpec((1, width, length), lambda p, me: (p, 0, 0)),
            scratch_shapes=[
                pltpu.VMEM((length, HEAD), BF),
                pltpu.VMEM((length, HEAD), BF),
                pltpu.VMEM((width, length), F32),
            ],
        ),
        out_shape=jax.ShapeDtypeStruct((count, width, length), BF),
        compiler_params=pltpu.CompilerParams(vmem_limit_bytes=40 << 20),
        cost_estimate=pl.CostEstimate(
            flops=count * 30 * GROUP * length * length * HEAD,
            bytes_accessed=count * length * 3000,
            transcendentals=count * GROUP * length * length // 2,
        ),
        name="attend_back",
    )(me, qkv, qkv, qkv, do, lse, delta, cos, sin)


def project_back(seq, me, pairs, xt, dr, w, gain, slices, earlier):
    length = xt.shape[2]
    span = length // slices
    width = (GROUP + 2) * HEAD
    tile = pl.BlockSpec((1, D, span), lambda k, me: (seq, 0, k ^ me[0]))
    return pl.pallas_call(
        project_back_kernel,
        grid_spec=pltpu.PrefetchScalarGridSpec(
            num_scalar_prefetch=1,
            grid=(slices,),
            in_specs=[
                *[pl.BlockSpec((1, width, span), lambda k, me, i=i: (i, 0, k ^ me[0])) for _, i in pairs],
                tile, tile, WHOLE, WHOLE, *[WHOLE] * len(earlier),
            ],
            out_specs=[pl.BlockSpec((1, D, span), lambda k, me: (k, 0, 0)), WHOLE, WHOLE],
            scratch_shapes=[pltpu.VMEM((8, D, 128), F32)],
        ),
        out_shape=[
            jax.ShapeDtypeStruct((slices, D, span), BF),
            jax.ShapeDtypeStruct((D * QKVW // 128, 128), F32),
            jax.ShapeDtypeStruct((D, 128), F32),
        ],
        compiler_params=pltpu.CompilerParams(vmem_limit_bytes=32 << 20),
        cost_estimate=pl.CostEstimate(
            flops=length * D * QKVW // 8, bytes_accessed=length * 500, transcendentals=0
        ),
        name="project_back",
    )(me, *[array for array, _ in pairs], xt, dr, w, gain, *earlier)


def partner(array, name, bits):
    return lax.ppermute(array, name, [(i, i ^ bits) for i in range(lax.axis_size(name))])


def digit_of(name, stride, count):
    return (lax.axis_index(name) // stride) % count


def in_order(parts, digit):
    bit = 1
    while bit < len(parts):
        swap = (digit & bit) != 0
        parts = [jnp.where(swap, parts[k ^ bit], parts[k]) for k in range(len(parts))]
        bit *= 2
    return parts


def after(value, *others):
    others = [other for other in others if other is not None]
    return lax.optimization_barrier((value, *others))[0] if others else value


def gather_digit(array, name, stride, count, hold=None):
    shape = array.shape
    step = 1
    while step < count:
        parts = [array, after(partner(array, name, step * stride), hold if 2 * step >= count else None)]
        array = jnp.stack(in_order(parts, digit_of(name, step * stride, 2)))
        step *= 2
    return array.reshape(count, *shape)


def sum_digit(terms, axis, name, stride, count, dtype, hold=None):
    digit = digit_of(name, stride, count)
    total = lax.dynamic_index_in_dim(terms, digit, axis, keepdims=False).astype(F32)
    for k in range(1, count):
        piece = lax.dynamic_index_in_dim(terms, digit ^ k, axis, keepdims=False).astype(BF)
        total = total + after(partner(piece, name, k * stride), hold).astype(F32)
    return total.astype(dtype)


def local(tokens, w_qkv, w_out, w_gate_up, w_down, gains, cotangent):
    slices = lax.axis_size("ctx")
    across = lax.axis_size("dp")
    world = slices * across
    span = tokens.shape[1]
    seqs = tokens.shape[0] // slices
    length = slices * span
    ctx = lax.axis_index("ctx")
    me = ctx.astype(jnp.int32).reshape(1)
    nz = min(4, across)
    nx = across // nz
    ny = slices // 2
    core = ("ctx", 1, 2)
    y = ("ctx", 2, ny)
    x = ("dp", 1, nx)
    z = ("dp", nx, nz)

    def blocks(array):
        grouped = array.transpose(0, 2, 1).reshape(slices, seqs, D, span)
        return [lax.dynamic_index_in_dim(grouped, ctx ^ k, 0, keepdims=False) for k in range(slices)]

    def receive(parts, hold, which):
        for k in which:
            parts[k] = after(partner(parts[k], "ctx", k), hold)
        return [parts[k] for k in which]

    everyone = range(1, slices)
    near = [k for k in everyone if k < 3]
    far = [k for k in everyone if k >= 3]

    def placed(stack):
        return stack.reshape(tokens.shape[0], D, span).transpose(0, 2, 1)

    def as_rows(shard):
        return jnp.pad(shard, (0, -shard.shape[0] % 1024)).reshape(-1, 128)

    def whole_flat(stack, order, size):
        stack = stack.transpose(*[order.index(d) for d in "zxyc"], 4, 5)
        return stack.reshape(world, -1, 128)[:, : -(-size // 128)].reshape(world, -1)[:, :size].reshape(-1, 128)

    def shares(flat):
        if flat.size % (world * 128) == 0:
            return flat.reshape(nz, nx, ny, 2, -1, 128)
        rows = flat.reshape(world, -1)
        return jnp.pad(rows, ((0, 0), (0, -rows.shape[1] % 128))).reshape(nz, nx, ny, 2, -1, 128)

    n_qkv = w_qkv.shape[0]
    n_gain = gains.shape[0]
    early = as_rows(jnp.concatenate([w_qkv, gains]))
    for digit in (y, x, z, core):
        early = gather_digit(early, *digit)
    early = early.transpose(1, 2, 3, 0, 4, 5).reshape(world, -1, 128)
    flat_qkv = early[:, : n_qkv // 128].reshape(-1, 128) if n_qkv % 128 == 0 else early.reshape(world, -1)[:, :n_qkv].reshape(-1, 128)
    gain_all = early.reshape(world, -1)[:, n_qkv : n_qkv + n_gain].reshape(2, D, 1).astype(F32)
    x_parts = blocks(tokens)
    receive(x_parts, None, everyone)
    gu_rows, down_rows = as_rows(w_gate_up), as_rows(w_down)
    rest1 = gather_digit(jnp.concatenate([gu_rows, down_rows, as_rows(w_out)]), *z, flat_qkv)
    gu1 = rest1[:, : gu_rows.shape[0]]
    both1 = rest1[:, gu_rows.shape[0] :]
    cos, sin = rotary_tables(length)
    mat_qkv, mat_qkv_t = prepare(flat_qkv)
    forward = ()
    dy_parts = blocks(after(cotangent, gu1, both1))
    for s in range(seqs):
        order = after(me, gu1, both1) if s == 0 else after(me, gu2, both2, *dy_near)
        forward = attention_forward(s, order, x_parts, mat_qkv_t, gain_all[0], cos, sin, forward)
        if s == 0:
            gu2 = gather_digit(gu1, *y, forward[3])
            both2 = gather_digit(both1, *x, forward[3])
            dy_near = receive(dy_parts, forward[3], near)
    xt, qkv, o, lse = forward
    gu3 = gather_digit(gu2, *x, lse)
    both3 = gather_digit(both2, *y, lse)
    flat_gu = whole_flat(gather_digit(gu3, *core, lse), "cxyz", w_gate_up.shape[0])
    both4 = gather_digit(both3, *core, lse)
    flat_down = whole_flat(both4[..., : down_rows.shape[0], :], "cyxz", w_down.shape[0])
    flat_out = whole_flat(both4[..., down_rows.shape[0] :, :], "cyxz", w_out.shape[0])
    receive(dy_parts, lse, far)
    dy_stack = jnp.stack(dy_parts)
    out_stack, dr, do, delta, g_out, g_gu, g_down, gg2 = middle(
        me, xt, o, dy_stack, flat_out, flat_gu, flat_down, gain_all[1]
    )

    n_pairs = seqs * KV_HEADS
    pairs = []
    back = []
    sums = [shares(g) for g in (g_gu, g_down, g_out)]
    gu_count, down_count = sums[0].shape[4], sums[1].shape[4]
    stages = [
        ((3, *core),) * 3,
        ((1, *x), (2, *y)),
        ((1, *y), (1, *x)),
    ]
    order = me
    out_parts = [out_stack[k] for k in range(slices)]
    out_waits = [near, far]

    def advance(hold):
        nonlocal sums
        if stages:
            sums = [sum_digit(r, *how, BF, hold) for r, how in zip(sums, stages.pop(0))]
            sums = [sums[0], jnp.concatenate(sums[1:], axis=-2)]
        return after(me, hold, *sums)

    for first in range(0, n_pairs, 2):
        count = min(2, n_pairs - first)
        dp = attend_back(first, count, order, qkv, do, lse, delta, cos, sin)
        pairs += [(dp, i) for i in range(count)]
        waited = receive(out_parts, dp, out_waits.pop(0)) if out_waits else []
        if first == 0 or n_pairs - first <= 2 or len(pairs) < KV_HEADS * (len(back) + 1):
            order = advance(dp)
        while len(pairs) >= KV_HEADS * (len(back) + 1):
            s = len(back)
            back.append(
                project_back(
                    s, order, pairs[KV_HEADS * s : KV_HEADS * (s + 1)], xt, dr, mat_qkv, gain_all[0], slices,
                    back[-1][1:] if back else (),
                )
            )
            if len(back) < seqs:
                order = advance(back[-1][2])
        order = after(order, *waited)
    while stages:
        advance(None)
    g_qkv, gg1 = back[-1][1:]
    returned = [[b[0][k] for k in range(slices)] for b in back]
    for parts in returned[:-1]:
        g_qkv = after(g_qkv, *receive(parts, gg1, everyone))
    gg = jnp.concatenate([jnp.sum(gg1, axis=1), jnp.sum(gg2, axis=1)])
    late = jnp.concatenate([g_qkv.reshape(world, -1), gg.reshape(world, -1)], axis=1)
    late = sum_digit(shares(late), 3, *core, BF)
    late = sum_digit(late, 1, *x, BF)
    late = sum_digit(late, 1, *y, BF)
    own_late = sum_digit(late, 0, *z, F32).reshape(-1)
    receive(returned[-1], late, everyone)
    own = jnp.concatenate(sums, axis=-2)
    step = nz // 2
    while step:
        own = own.reshape(2, step, *own.shape[1:])
        own = sum_digit(own, 0, "dp", nx * step, 2, BF if step > 1 else F32, late)
        step //= 2
    own = own.reshape(own.shape[-2:])
    out_parts[0] = after(out_parts[0], late)
    output = placed(jnp.stack(in_order(out_parts, ctx)))
    grad_input = placed(jnp.stack([jnp.stack(in_order(parts, ctx)) for parts in returned], axis=1))
    return (
        output,
        grad_input,
        own_late[:n_qkv],
        own[gu_count + down_count :].reshape(-1)[: w_out.shape[0]],
        own[:gu_count].reshape(-1)[: w_gate_up.shape[0]],
        own[gu_count : gu_count + down_count].reshape(-1)[: w_down.shape[0]],
        own_late[n_qkv : n_qkv + n_gain],
    )


def solution(mesh):
    flat = P(("dp", "ctx"))
    rows = P("dp", "ctx", None)
    return jax.shard_map(
        local,
        mesh=mesh,
        in_specs=(rows, flat, flat, flat, flat, flat, rows),
        out_specs=(rows, rows, flat, flat, flat, flat, flat),
        check_vma=False,
    )
```

```python
import functools
import math

import jax
import jax.numpy as jnp
from jax import lax
from jax.experimental import pallas as pl
from jax.experimental.pallas import tpu as pltpu
from jax.sharding import PartitionSpec as P

D = 576
HEADS = 9
KV_HEADS = 3
HEAD = 64
GROUP = HEADS // KV_HEADS
FF = 1536
QKVW = 960
KV0 = D
V0 = D + KV_HEADS * HEAD
HALF = HEAD // 2
TILE = 256

EPSILON = 1e-05
THETA_BASE = 100000.0
NEG_FILL = -1e30
BF = jnp.bfloat16
F32 = jnp.float32


def nn(a, b):
    return lax.dot_general(a, b, (((1,), (0,)), ((), ())), preferred_element_type=F32)


def nt(a, b):
    return lax.dot_general(a, b, (((1,), (1,)), ((), ())), preferred_element_type=F32)


def eye(size):
    r = lax.broadcasted_iota(jnp.int32, (size, size), 0)
    c = lax.broadcasted_iota(jnp.int32, (size, size), 1)
    return jnp.where(r == c, 1.0, 0.0).astype(BF)


def col_chunks(width, step=128):
    return [(c, min(step, width - c)) for c in range(0, width, step)]


def unflip(cols):
    return nt(eye(cols.shape[1]), cols).astype(BF)


def inverse_rms(cols):
    return lax.rsqrt(jnp.sum(cols * cols, axis=0, keepdims=True) * (1.0 / D) + EPSILON)


def rotary_tables(length):
    halves = jnp.arange(0, HEAD, 2).astype(F32) / HEAD
    inverse = jnp.exp(-math.log(THETA_BASE) * halves)
    angles = inverse[:, None] * jnp.arange(length).astype(F32)[None, :]
    return jnp.cos(angles), jnp.sin(angles)


def tri_mask(size):
    key = lax.broadcasted_iota(jnp.int32, (size, size), 0)
    query = lax.broadcasted_iota(jnp.int32, (size, size), 1)
    return key <= query


def lane_low(size):
    return lax.broadcasted_iota(jnp.int32, (size, 128), 1) < 64


def to_flat(rows_ref, flat_ref, rows, width):
    if width % 128 == 0:
        n = width // 128

        @pl.loop(0, n)
        def _(c):
            flat_ref[pl.ds(c, rows, stride=n), :] = rows_ref[:, pl.ds(pl.multiple_of(c * 128, 128), 128)]

        return
    n = 2 * width // 128
    half = rows // 2
    low = lane_low(half)
    even = lambda c: rows_ref[c, pl.ds(0, half, stride=2), :]
    odd = lambda c: pltpu.roll(rows_ref[c, pl.ds(1, half, stride=2), :], 64, 1)
    for c in range(n // 2):
        flat_ref[pl.ds(c, half, stride=n), :] = even(c)
    before = odd(0)
    flat_ref[pl.ds(n // 2, half, stride=n), :] = jnp.where(low, even(n // 2), before)
    for c in range(n // 2):
        after = odd(c + 1)
        flat_ref[pl.ds(n // 2 + 1 + c, half, stride=n), :] = jnp.where(low, before, after)
        before = after


def from_flat(flat_ref, rows_ref, rows, width):
    if width % 128 == 0:
        n = width // 128

        @pl.loop(0, n)
        def _(c):
            rows_ref[:, pl.ds(pl.multiple_of(c * 128, 128), 128)] = flat_ref[
                pl.ds(c, rows, stride=n), :
            ].astype(rows_ref.dtype)

        return
    n = 2 * width // 128
    half = rows // 2
    low = lane_low(half)
    take = lambda c: flat_ref[pl.ds(c, half, stride=n), :]
    for c in range(n // 2 + 1):
        rows_ref[c, pl.ds(0, half, stride=2), :] = take(c)
    before = pltpu.roll(take(n // 2), 64, 1)
    for c in range(n // 2):
        after = pltpu.roll(take(n // 2 + 1 + c), 64, 1)
        rows_ref[c, pl.ds(1, half, stride=2), :] = jnp.where(low, before, after)
        before = after
    rows_ref[n // 2, pl.ds(1, half, stride=2), :] = before


def convert(src_ref, dst_ref, rows, step):
    @pl.loop(0, rows, step=step)
    def _(i):
        at = pl.ds(pl.multiple_of(i, step), step)
        dst_ref[at, :] = src_ref[at, 0 : dst_ref.shape[1]].astype(dst_ref.dtype)


def clear(ref, step):
    @pl.loop(0, ref.shape[-2], step=step)
    def _(i):
        at = pl.ds(pl.multiple_of(i, step), step)
        if len(ref.shape) == 3:
            ref[:, at, :] = jnp.zeros((ref.shape[0], step, ref.shape[2]), ref.dtype)
        else:
            ref[at, :] = jnp.zeros((step, ref.shape[1]), ref.dtype)


def add_chunks(ref, value):
    for c, w in col_chunks(value.shape[1]):
        ref[c // 128, :, 0:w] += value[:, c : c + w]


def join_chunks(src_ref, dst_ref):
    for c, w in col_chunks(dst_ref.shape[1]):
        dst_ref[:, c : c + w] = src_ref[c // 128, :, 0:w].astype(dst_ref.dtype)


def prepare_kernel(flat_ref, w_ref, wt_ref, flat, rows):
    convert(flat_ref, flat, flat.shape[0], 240)
    from_flat(flat, rows, D, QKVW)
    join_chunks(rows, w_ref)
    for c, w in col_chunks(QKVW):
        wt_ref[c : c + w, :] = nt(eye(w), w_ref[:, c : c + w]).astype(BF)


def forward_kernel(slices, me_ref, *refs):
    x_refs = refs[:slices]
    wt_ref, gain_ref, cos_ref, sin_ref = refs[slices : slices + 4]
    xt_ref, qkv_ref, o_ref, lse_ref, krow = refs[-5:]
    _, _, span = x_refs[0].shape
    length = slices * span
    me = me_ref[0]
    for k in range(slices):
        at = pl.multiple_of((me ^ k) * span, span)
        xt_ref[0, :, pl.ds(at, span)] = x_refs[k][0]
    gain = gain_ref[...]

    @pl.loop(0, length, step=TILE)
    def _(start):
        tok = pl.ds(pl.multiple_of(start, TILE), TILE)
        x = xt_ref[0, :, tok].astype(F32)
        normed = (x * inverse_rms(x) * gain).astype(BF)
        proj = nn(wt_ref[...], normed)
        cos = cos_ref[:, tok]
        sin = sin_ref[:, tok]
        for j in range(HEADS + KV_HEADS):
            u1 = proj[j * HEAD : j * HEAD + HALF]
            u2 = proj[j * HEAD + HALF : (j + 1) * HEAD]
            r1 = (u1 * cos - u2 * sin).astype(BF)
            r2 = (u2 * cos + u1 * sin).astype(BF)
            if j < HEADS:
                r1 = r1 * jnp.asarray(0.125, BF)
                r2 = r2 * jnp.asarray(0.125, BF)
            qkv_ref[0, j * HEAD : j * HEAD + HALF, tok] = r1
            qkv_ref[0, j * HEAD + HALF : (j + 1) * HEAD, tok] = r2
        qkv_ref[0, V0:, tok] = proj[V0:].astype(BF)
        for j in range(KV_HEADS):
            krow[j, tok, :] = unflip(qkv_ref[0, KV0 + j * HEAD : KV0 + (j + 1) * HEAD, tok])

    keep = tri_mask(TILE)

    def head(h, carry):
        kv = h // GROUP
        rows = pl.ds(pl.multiple_of(h * HEAD, HEAD), HEAD)
        vrows = pl.ds(pl.multiple_of(V0 + kv * HEAD, HEAD), HEAD)
        for t in range(0, length, TILE):
            cols = slice(t, t + TILE)
            q = qkv_ref[0, rows, cols]
            last = jnp.where(keep, nn(krow[kv, cols, :], q), NEG_FILL)
            top = jnp.max(last, axis=0, keepdims=True)
            if t:
                before = nn(krow[kv, 0:t, :], q)
                top = jnp.maximum(top, jnp.max(before, axis=0, keepdims=True))
            e = jnp.exp(last - top)
            total = jnp.sum(e, axis=0, keepdims=True)
            acc = nn(qkv_ref[0, vrows, cols], e.astype(BF))
            if t:
                e = jnp.exp(before - top)
                total = total + jnp.sum(e, axis=0, keepdims=True)
                acc = acc + nn(qkv_ref[0, vrows, 0:t], e.astype(BF))
            o_ref[0, rows, cols] = (acc * (1.0 / total)).astype(BF)
            lse_ref[0, kv, pl.ds(h % GROUP, 1), cols] = top + jnp.log(total)
        return carry

    lax.fori_loop(0, HEADS, head, 0)


def middle_kernel(
    me_ref, xt_ref, o_ref, dy_ref, fo_ref, fgu_ref, fd_ref, gain_ref,
    out_ref, dr_ref, do_ref, delta_ref, gout_ref, ggu_ref, gdown_ref, gg_ref,
    wo_ref, wgu_ref, wd_ref, wot, wgut, wdt, aout, agu, adown,
):
    step = pl.program_id(0) * pl.num_programs(1) + pl.program_id(1)
    last = pl.num_programs(0) * pl.num_programs(1) - 1

    @pl.when(step == 0)
    def _():
        convert(fgu_ref, ggu_ref, fgu_ref.shape[0], 256)
        from_flat(ggu_ref, wgu_ref, D, 2 * FF)
        convert(fd_ref, gdown_ref, fd_ref.shape[0], 256)
        from_flat(gdown_ref, adown, FF, D)
        join_chunks(adown, wd_ref)
        convert(fo_ref, gout_ref, fo_ref.shape[0], 96)
        from_flat(gout_ref, aout, D, D)
        join_chunks(aout, wo_ref)

        @pl.loop(0, 2 * FF, step=TILE)
        def _(c):
            at = pl.ds(pl.multiple_of(c, TILE), TILE)
            wgut[at, :] = nt(eye(TILE), wgu_ref[:, at]).astype(BF)

        for c, w in col_chunks(D):
            wdt[c : c + w, :] = nt(eye(w), wd_ref[:, c : c + w]).astype(BF)
            wot[c : c + w, :] = nt(eye(w), wo_ref[:, c : c + w]).astype(BF)
        clear(aout, 64)
        clear(agu, 16)
        clear(adown, 64)
        gg_ref[...] = jnp.zeros_like(gg_ref)

    gain = gain_ref[...]
    o = o_ref[0]
    r = xt_ref[0].astype(F32) + nn(wot[...], o)
    inv = inverse_rms(r)
    n = r * inv
    h = (n * gain).astype(BF)
    a = nn(wgut[0:FF, :], h)
    u = nn(wgut[FF:, :], h)
    sg = 1.0 / (1.0 + jnp.exp(-a))
    act = a * sg
    m = (act * u).astype(BF)
    out_ref[0, 0] = (r + nn(wdt[...], m)).astype(BF)
    dyt = dy_ref[0, 0]
    add_chunks(adown, nt(m, dyt))
    dm = nn(wd_ref[...], dyt)
    da = (dm * u * sg * (1.0 + a * (1.0 - sg))).astype(BF)
    du = (dm * act).astype(BF)
    agu[:, 0:FF] += nt(h, da)
    agu[:, FF:] += nt(h, du)
    dh = nn(wgu_ref[:, 0:FF], da) + nn(wgu_ref[:, FF:], du)
    dhn = dh * n
    part = dhn[:, 0:128]
    for c in range(128, dhn.shape[1], 128):
        part = part + dhn[:, c : c + 128]
    gg_ref[...] += part
    e = dh * gain
    dr = dyt.astype(F32) + inv * (e - n * (jnp.sum(e * n, axis=0, keepdims=True) * (1.0 / D)))
    dr_ref[0] = dr.astype(BF)
    db = dr.astype(BF)
    add_chunks(aout, nt(o, db))
    do = nn(wo_ref[...], db).astype(BF)
    do_ref[0] = do
    prod = do.astype(F32) * o.astype(F32)
    for j in range(HEADS):
        delta_ref[0, j // GROUP, j % GROUP : j % GROUP + 1, :] = jnp.sum(prod[j * HEAD : (j + 1) * HEAD], axis=0, keepdims=True)

    @pl.when(step == last)
    def _():
        to_flat(aout, gout_ref, D, D)
        to_flat(agu, ggu_ref, D, 2 * FF)
        to_flat(adown, gdown_ref, FF, D)


def attend_back_kernel(
    me_ref, q_ref, k_ref, v_ref, do_ref, lse_ref, delta_ref, cos_ref, sin_ref, dp_ref, krow, vrow, grads
):
    length = q_ref.shape[2]
    k0 = GROUP * HEAD
    v0 = k0 + HEAD
    clear(grads, 64)

    @pl.loop(0, length, step=TILE)
    def _(start):
        tok = pl.ds(pl.multiple_of(start, TILE), TILE)
        krow[tok, :] = unflip(k_ref[0, :, tok])
        vrow[tok, :] = unflip(v_ref[0, :, tok])

    keep = tri_mask(TILE)

    def head(h, carry):
        rows = pl.ds(pl.multiple_of(h * HEAD, HEAD), HEAD)
        for t in range(0, length, TILE):
            cols = slice(t, t + TILE)
            q = q_ref[0, rows, cols]
            do = do_ref[0, rows, cols]
            lse = lse_ref[0, 0, pl.ds(h, 1), cols]
            delta = delta_ref[0, 0, pl.ds(h, 1), cols]
            p = jnp.where(keep, jnp.exp(nn(krow[cols, :], q) - lse), 0.0)
            ds = (p * (nn(vrow[cols, :], do) - delta)).astype(BF)
            grads[v0:, cols] += nt(do, p.astype(BF))
            grads[k0:v0, cols] += nt(q, ds)
            dq = nn(k_ref[0, :, cols], ds)
            if t:
                p = jnp.exp(nn(krow[0:t, :], q) - lse)
                ds = (p * (nn(vrow[0:t, :], do) - delta)).astype(BF)
                grads[v0:, 0:t] += nt(do, p.astype(BF))
                grads[k0:v0, 0:t] += nt(q, ds)
                dq = dq + nn(k_ref[0, :, 0:t], ds)
            grads[rows, cols] = dq * 0.125
        return carry

    lax.fori_loop(0, GROUP, head, 0)

    @pl.loop(0, length, step=TILE)
    def _(start):
        tok = pl.ds(pl.multiple_of(start, TILE), TILE)
        cos = cos_ref[:, tok]
        sin = sin_ref[:, tok]
        for j in range(GROUP + 1):
            one = slice(j * HEAD, j * HEAD + HALF)
            two = slice(j * HEAD + HALF, (j + 1) * HEAD)
            g1 = grads[one, tok]
            g2 = grads[two, tok]
            dp_ref[0, one, tok] = (g1 * cos + g2 * sin).astype(BF)
            dp_ref[0, two, tok] = (g2 * cos - g1 * sin).astype(BF)
        dp_ref[0, v0:, tok] = grads[v0:, tok].astype(BF)


def project_back_kernel(me_ref, d0_ref, d1_ref, d2_ref, xt_ref, dr_ref, w_ref, gain_ref, *refs):
    gin_ref, gqkv_ref, gg_ref, acc = refs[-4:]

    @pl.when(pl.program_id(0) == 0)
    def _():
        if len(refs) > 4:
            from_flat(refs[0], acc, D, QKVW)
            gg_ref[...] = refs[1][...]
        else:
            clear(acc, 64)
            gg_ref[...] = jnp.zeros_like(gg_ref)

    groups = (d0_ref, d1_ref, d2_ref)
    k0 = GROUP * HEAD
    v0 = k0 + HEAD
    dp = jnp.concatenate(
        [g[0, 0:k0, :] for g in groups] + [g[0, k0:v0, :] for g in groups] + [g[0, v0:, :] for g in groups], axis=0
    )
    x = xt_ref[0].astype(F32)
    inv = inverse_rms(x)
    n = x * inv
    gain = gain_ref[...]
    add_chunks(acc, nt((n * gain).astype(BF), dp))
    dh = nn(w_ref[...], dp)
    dhn = dh * n
    part = dhn[:, 0:128]
    for c in range(128, dhn.shape[1], 128):
        part = part + dhn[:, c : c + 128]
    gg_ref[...] += part
    e = dh * gain
    gin = dr_ref[0].astype(F32) + inv * (e - n * (jnp.sum(e * n, axis=0, keepdims=True) * (1.0 / D)))
    gin_ref[0] = gin.astype(BF)

    @pl.when(pl.program_id(0) == pl.num_programs(0) - 1)
    def _():
        to_flat(acc, gqkv_ref, D, QKVW)


WHOLE = pl.BlockSpec(memory_space=pltpu.VMEM)


def prepare(flat):
    return pl.pallas_call(
        prepare_kernel,
        in_specs=[WHOLE],
        out_specs=[WHOLE, WHOLE],
        out_shape=[jax.ShapeDtypeStruct((D, QKVW), BF), jax.ShapeDtypeStruct((QKVW, D), BF)],
        scratch_shapes=[pltpu.VMEM(flat.shape, F32), pltpu.VMEM((8, D, 128), F32)],
        compiler_params=pltpu.CompilerParams(vmem_limit_bytes=24 << 20),
        cost_estimate=pl.CostEstimate(flops=2 * D * D * QKVW, bytes_accessed=6 * D * QKVW, transcendentals=0),
        name="prepare",
    )(flat)


def attention_forward(seq, me, x_parts, wt, gain, cos, sin, before):
    slices = len(x_parts)
    seqs, _, span = x_parts[0].shape
    length = slices * span
    by_seq = lambda rows: pl.BlockSpec((1, rows, length), lambda s, me: (seq, 0, 0))
    stats = pl.BlockSpec((1, KV_HEADS, GROUP, length), lambda s, me: (seq, 0, 0, 0))
    n_in = 1 + slices + 4
    return pl.pallas_call(
        functools.partial(forward_kernel, slices),
        grid_spec=pltpu.PrefetchScalarGridSpec(
            num_scalar_prefetch=1,
            grid=(1,),
            in_specs=[
                *[pl.BlockSpec((1, D, span), lambda s, me: (seq, 0, 0))] * slices,
                WHOLE, WHOLE, WHOLE, WHOLE,
                *[pl.BlockSpec(memory_space=pl.ANY)] * len(before),
            ],
            out_specs=[by_seq(D), by_seq(QKVW), by_seq(D), stats],
            scratch_shapes=[pltpu.VMEM((KV_HEADS, length, HEAD), BF)],
        ),
        out_shape=[
            jax.ShapeDtypeStruct((seqs, D, length), BF),
            jax.ShapeDtypeStruct((seqs, QKVW, length), BF),
            jax.ShapeDtypeStruct((seqs, D, length), BF),
            jax.ShapeDtypeStruct((seqs, KV_HEADS, GROUP, length), F32),
        ],
        input_output_aliases={n_in + i: i for i in range(len(before))},
        compiler_params=pltpu.CompilerParams(vmem_limit_bytes=40 << 20),
        cost_estimate=pl.CostEstimate(
            flops=2 * length * D * QKVW + 16 * HEADS * length * length * HEAD,
            bytes_accessed=length * 7000,
            transcendentals=HEADS * length * length // 2,
        ),
        name="attention_forward",
    )(me, *x_parts, wt, gain, cos, sin, *before)


def middle(me, xt, o, dy_stack, wo, wgu, wd, gain):
    slices, seqs, _, span = dy_stack.shape
    length = slices * span
    stats = pl.BlockSpec((1, KV_HEADS, GROUP, span), lambda s, k, me: (s, 0, 0, k ^ me[0]))
    tile = lambda rows: pl.BlockSpec((1, rows, span), lambda s, k, me: (s, 0, k ^ me[0]))
    stacked = pl.BlockSpec((1, 1, D, span), lambda s, k, me: (k, s, 0, 0))
    return pl.pallas_call(
        middle_kernel,
        grid_spec=pltpu.PrefetchScalarGridSpec(
            num_scalar_prefetch=1,
            grid=(seqs, slices),
            in_specs=[tile(D), tile(D), stacked, WHOLE, WHOLE, WHOLE, WHOLE],
            out_specs=[stacked, tile(D), tile(D), stats, WHOLE, WHOLE, WHOLE, WHOLE],
            scratch_shapes=[
                pltpu.VMEM((D, D), BF),
                pltpu.VMEM((D, 2 * FF), BF),
                pltpu.VMEM((FF, D), BF),
                pltpu.VMEM((D, D), BF),
                pltpu.VMEM((2 * FF, D), BF),
                pltpu.VMEM((D, FF), BF),
                pltpu.VMEM((5, D, 128), F32),
                pltpu.VMEM((D, 2 * FF), F32),
                pltpu.VMEM((5, FF, 128), F32),
            ],
        ),
        out_shape=[
            jax.ShapeDtypeStruct((slices, seqs, D, span), BF),
            jax.ShapeDtypeStruct((seqs, D, length), BF),
            jax.ShapeDtypeStruct((seqs, D, length), BF),
            jax.ShapeDtypeStruct((seqs, KV_HEADS, GROUP, length), F32),
            jax.ShapeDtypeStruct((D * D // 128, 128), F32),
            jax.ShapeDtypeStruct((D * 2 * FF // 128, 128), F32),
            jax.ShapeDtypeStruct((FF * D // 128, 128), F32),
            jax.ShapeDtypeStruct((D, 128), F32),
        ],
        compiler_params=pltpu.CompilerParams(vmem_limit_bytes=60 << 20),
        cost_estimate=pl.CostEstimate(
            flops=seqs * length * 6 * (D * D + 3 * D * FF),
            bytes_accessed=seqs * length * 8000 + 12000000,
            transcendentals=seqs * length * FF,
        ),
        name="middle",
    )(me, xt, o, dy_stack, wo, wgu, wd, gain)


def attend_back(first, count, me, qkv, do, lse, delta, cos, sin):
    length = qkv.shape[2]
    width = (GROUP + 2) * HEAD
    at = lambda p: ((first + p) // KV_HEADS, (first + p) % KV_HEADS)
    rows = lambda n, base: pl.BlockSpec((1, n, length), lambda p, me: (at(p)[0], base + at(p)[1], 0))
    stats = pl.BlockSpec((1, 1, GROUP, length), lambda p, me: (*at(p), 0, 0))
    return pl.pallas_call(
        attend_back_kernel,
        grid_spec=pltpu.PrefetchScalarGridSpec(
            num_scalar_prefetch=1,
            grid=(count,),
            in_specs=[
                rows(GROUP * HEAD, 0), rows(HEAD, KV0 // HEAD), rows(HEAD, V0 // HEAD), rows(GROUP * HEAD, 0),
                stats, stats, WHOLE, WHOLE,
            ],
            out_specs=pl.BlockSpec((1, width, length), lambda p, me: (p, 0, 0)),
            scratch_shapes=[
                pltpu.VMEM((length, HEAD), BF),
                pltpu.VMEM((length, HEAD), BF),
                pltpu.VMEM((width, length), F32),
            ],
        ),
        out_shape=jax.ShapeDtypeStruct((count, width, length), BF),
        compiler_params=pltpu.CompilerParams(vmem_limit_bytes=40 << 20),
        cost_estimate=pl.CostEstimate(
            flops=count * 30 * GROUP * length * length * HEAD,
            bytes_accessed=count * length * 3000,
            transcendentals=count * GROUP * length * length // 2,
        ),
        name="attend_back",
    )(me, qkv, qkv, qkv, do, lse, delta, cos, sin)


def project_back(seq, me, pairs, xt, dr, w, gain, slices, earlier):
    length = xt.shape[2]
    span = length // slices
    width = (GROUP + 2) * HEAD
    tile = pl.BlockSpec((1, D, span), lambda k, me: (seq, 0, k ^ me[0]))
    return pl.pallas_call(
        project_back_kernel,
        grid_spec=pltpu.PrefetchScalarGridSpec(
            num_scalar_prefetch=1,
            grid=(slices,),
            in_specs=[
                *[pl.BlockSpec((1, width, span), lambda k, me, i=i: (i, 0, k ^ me[0])) for _, i in pairs],
                tile, tile, WHOLE, WHOLE, *[WHOLE] * len(earlier),
            ],
            out_specs=[pl.BlockSpec((1, D, span), lambda k, me: (k, 0, 0)), WHOLE, WHOLE],
            scratch_shapes=[pltpu.VMEM((8, D, 128), F32)],
        ),
        out_shape=[
            jax.ShapeDtypeStruct((slices, D, span), BF),
            jax.ShapeDtypeStruct((D * QKVW // 128, 128), F32),
            jax.ShapeDtypeStruct((D, 128), F32),
        ],
        compiler_params=pltpu.CompilerParams(vmem_limit_bytes=32 << 20),
        cost_estimate=pl.CostEstimate(
            flops=8 * length * D * QKVW, bytes_accessed=length * 8000 + 4000000, transcendentals=0
        ),
        name="project_back",
    )(me, *[array for array, _ in pairs], xt, dr, w, gain, *earlier)


def partner(array, name, bits):
    return lax.ppermute(array, name, [(i, i ^ bits) for i in range(lax.axis_size(name))])


def digit_of(name, stride, count):
    return (lax.axis_index(name) // stride) % count


def in_order(parts, digit):
    bit = 1
    while bit < len(parts):
        swap = (digit & bit) != 0
        parts = [jnp.where(swap, parts[k ^ bit], parts[k]) for k in range(len(parts))]
        bit *= 2
    return parts


def after(value, *others):
    others = [other for other in others if other is not None]
    return lax.optimization_barrier((value, *others))[0] if others else value


def gather_digit(array, name, stride, count, hold=None):
    shape = array.shape
    step = 1
    while step < count:
        parts = [array, after(partner(array, name, step * stride), hold if 2 * step >= count else None)]
        array = jnp.stack(in_order(parts, digit_of(name, step * stride, 2)))
        step *= 2
    return array.reshape(count, *shape)


def sum_digit(terms, axis, name, stride, count, dtype, hold=None):
    digit = digit_of(name, stride, count)
    total = lax.dynamic_index_in_dim(terms, digit, axis, keepdims=False).astype(F32)
    for k in range(1, count):
        piece = lax.dynamic_index_in_dim(terms, digit ^ k, axis, keepdims=False).astype(BF)
        total = total + after(partner(piece, name, k * stride), hold).astype(F32)
    return total.astype(dtype)


def local(tokens, w_qkv, w_out, w_gate_up, w_down, gains, cotangent):
    slices = lax.axis_size("ctx")
    across = lax.axis_size("dp")
    world = slices * across
    span = tokens.shape[1]
    seqs = tokens.shape[0] // slices
    length = slices * span
    ctx = lax.axis_index("ctx")
    me = ctx.astype(jnp.int32).reshape(1)
    nz = min(4, across)
    nx = across // nz
    ny = slices // 2
    core = ("ctx", 1, 2)
    y = ("ctx", 2, ny)
    x = ("dp", 1, nx)
    z = ("dp", nx, nz)

    def blocks(array):
        grouped = array.transpose(0, 2, 1).reshape(slices, seqs, D, span)
        return [lax.dynamic_index_in_dim(grouped, ctx ^ k, 0, keepdims=False) for k in range(slices)]

    def receive(parts, hold, which):
        for k in which:
            parts[k] = after(partner(parts[k], "ctx", k), hold)
        return [parts[k] for k in which]

    everyone = range(1, slices)
    near = [k for k in everyone if k < 3]
    far = [k for k in everyone if k >= 3]

    def placed(stack):
        return stack.reshape(tokens.shape[0], D, span).transpose(0, 2, 1)

    def as_rows(shard):
        return jnp.pad(shard, (0, -shard.shape[0] % 1024)).reshape(-1, 128)

    def whole_flat(stack, order, size):
        stack = stack.transpose(*[order.index(d) for d in "zxyc"], 4, 5)
        return stack.reshape(world, -1, 128)[:, : -(-size // 128)].reshape(world, -1)[:, :size].reshape(-1, 128)

    def shares(flat):
        if flat.size % (world * 128) == 0:
            return flat.reshape(nz, nx, ny, 2, -1, 128)
        rows = flat.reshape(world, -1)
        return jnp.pad(rows, ((0, 0), (0, -rows.shape[1] % 128))).reshape(nz, nx, ny, 2, -1, 128)

    n_qkv = w_qkv.shape[0]
    n_gain = gains.shape[0]
    early = as_rows(jnp.concatenate([w_qkv, gains]))
    for digit in (y, x, z, core):
        early = gather_digit(early, *digit)
    early = early.transpose(1, 2, 3, 0, 4, 5).reshape(world, -1, 128)
    flat_qkv = early[:, : n_qkv // 128].reshape(-1, 128) if n_qkv % 128 == 0 else early.reshape(world, -1)[:, :n_qkv].reshape(-1, 128)
    gain_all = early.reshape(world, -1)[:, n_qkv : n_qkv + n_gain].reshape(2, D, 1).astype(F32)
    x_parts = blocks(tokens)
    receive(x_parts, None, everyone)
    gu_rows, down_rows = as_rows(w_gate_up), as_rows(w_down)
    rest1 = gather_digit(jnp.concatenate([gu_rows, down_rows, as_rows(w_out)]), *z, flat_qkv)
    gu1 = rest1[:, : gu_rows.shape[0]]
    both1 = rest1[:, gu_rows.shape[0] :]
    cos, sin = rotary_tables(length)
    mat_qkv, mat_qkv_t = prepare(flat_qkv)
    forward = ()
    dy_parts = blocks(after(cotangent, gu1, both1))
    for s in range(seqs):
        order = after(me, gu1, both1) if s == 0 else after(me, gu2, both2, *dy_near)
        forward = attention_forward(s, order, x_parts, mat_qkv_t, gain_all[0], cos, sin, forward)
        if s == 0:
            gu2 = gather_digit(gu1, *y, forward[3])
            both2 = gather_digit(both1, *x, forward[3])
            dy_near = receive(dy_parts, forward[3], near)
    xt, qkv, o, lse = forward
    gu3 = gather_digit(gu2, *x, lse)
    both3 = gather_digit(both2, *y, lse)
    flat_gu = whole_flat(gather_digit(gu3, *core, lse), "cxyz", w_gate_up.shape[0])
    both4 = gather_digit(both3, *core, lse)
    flat_down = whole_flat(both4[..., : down_rows.shape[0], :], "cyxz", w_down.shape[0])
    flat_out = whole_flat(both4[..., down_rows.shape[0] :, :], "cyxz", w_out.shape[0])
    receive(dy_parts, lse, far)
    dy_stack = jnp.stack(dy_parts)
    out_stack, dr, do, delta, g_out, g_gu, g_down, gg2 = middle(
        me, xt, o, dy_stack, flat_out, flat_gu, flat_down, gain_all[1]
    )

    n_pairs = seqs * KV_HEADS
    pairs = []
    back = []
    sums = [shares(g) for g in (g_gu, g_down, g_out)]
    gu_count, down_count = sums[0].shape[4], sums[1].shape[4]
    stages = [
        ((3, *core),) * 3,
        ((1, *x), (2, *y)),
        ((1, *y), (1, *x)),
    ]
    order = me
    out_parts = [out_stack[k] for k in range(slices)]
    out_waits = [near, far]

    def advance(hold):
        nonlocal sums
        if stages:
            sums = [sum_digit(r, *how, BF, hold) for r, how in zip(sums, stages.pop(0))]
            sums = [sums[0], jnp.concatenate(sums[1:], axis=-2)]
        return after(me, hold, *sums)

    for first in range(0, n_pairs, 2):
        count = min(2, n_pairs - first)
        dp = attend_back(first, count, order, qkv, do, lse, delta, cos, sin)
        pairs += [(dp, i) for i in range(count)]
        waited = receive(out_parts, dp, out_waits.pop(0)) if out_waits else []
        if first == 0 or n_pairs - first <= 2 or len(pairs) < KV_HEADS * (len(back) + 1):
            order = advance(dp)
        while len(pairs) >= KV_HEADS * (len(back) + 1):
            s = len(back)
            back.append(
                project_back(
                    s, order, pairs[KV_HEADS * s : KV_HEADS * (s + 1)], xt, dr, mat_qkv, gain_all[0], slices,
                    back[-1][1:] if back else (),
                )
            )
            if len(back) < seqs:
                order = advance(back[-1][2])
        order = after(order, *waited)
    while stages:
        advance(None)
    g_qkv, gg1 = back[-1][1:]
    returned = [[b[0][k] for k in range(slices)] for b in back]
    for parts in returned[:-1]:
        g_qkv = after(g_qkv, *receive(parts, gg1, everyone))
    gg = jnp.concatenate([jnp.sum(gg1, axis=1), jnp.sum(gg2, axis=1)])
    late = jnp.concatenate([g_qkv.reshape(world, -1), gg.reshape(world, -1)], axis=1)
    late = sum_digit(shares(late), 3, *core, BF)
    late = sum_digit(late, 1, *x, BF)
    late = sum_digit(late, 1, *y, BF)
    own_late = sum_digit(late, 0, *z, F32).reshape(-1)
    receive(returned[-1], late, everyone)
    own = jnp.concatenate(sums, axis=-2)
    step = nz // 2
    while step:
        own = own.reshape(2, step, *own.shape[1:])
        own = sum_digit(own, 0, "dp", nx * step, 2, BF if step > 1 else F32, late)
        step //= 2
    own = own.reshape(own.shape[-2:])
    out_parts[0] = after(out_parts[0], late)
    output = placed(jnp.stack(in_order(out_parts, ctx)))
    grad_input = placed(jnp.stack([jnp.stack(in_order(parts, ctx)) for parts in returned], axis=1))
    return (
        output,
        grad_input,
        own_late[:n_qkv],
        own[gu_count + down_count :].reshape(-1)[: w_out.shape[0]],
        own[:gu_count].reshape(-1)[: w_gate_up.shape[0]],
        own[gu_count : gu_count + down_count].reshape(-1)[: w_down.shape[0]],
        own_late[n_qkv : n_qkv + n_gain],
    )


def solution(mesh):
    flat = P(("dp", "ctx"))
    rows = P("dp", "ctx", None)
    return jax.shard_map(
        local,
        mesh=mesh,
        in_specs=(rows, flat, flat, flat, flat, flat, rows),
        out_specs=(rows, rows, flat, flat, flat, flat, flat),
        check_vma=False,
    )
```
